32 devices in a mesh: groups: 2 (over x), tensor: 16 (over z, y, core).
Axes of the slice: x: 2, y: 2, z: 4, core: 2. Of those that a mesh axis runs over, the one named last changes fastest.
Arguments:
- queries: bfloat16 [16, 16384], P('groups', 'tensor'), parts along dimension 0, may hold values from -120 to 120
- kv_cache: bfloat16 [2, 16, 512, 1024], P(None, 'groups', 'tensor'), parts along dimension 1, may hold values from -4 to 4
- lengths: int32 [16], P('groups'), parts along dimension 0, may hold values from 2 to 512, as said below
- out_weight: bfloat16 [16384, 16384], P('tensor'), may hold values from -0.8984375 to 0.8984375
- outlier_values: bfloat16 [128, 4, 128, 128], P('tensor'), may hold values from -3 to 3
- outlier_columns: int32 [128, 4], P('tensor'), may hold values from 0 to 127
- outlier_counts: int32 [128], P('tensor'), may hold values from 1 to 4, as said below
Outputs:
- mixed: bfloat16 [16, 16384], P('groups', 'tensor'), parts along dimension 0
The draws below stay inside these ranges and needn't reach their ends.
There are 2 independent parts, one for each index of `groups`. The reference program is written for one: setup_inputs(seed, part) draws one part's arguments, and reference() takes and returns one part's arrays. A program takes and returns all parts, laid end to end along the dimension named above; an argument that names none is the same for every part. Nothing has to cross between parts.
Inputs may be any that keep to these rules, and one draw needn't show every extreme that they name: `lengths`: some request has all 512 positions live and some has 2. `outlier_counts`: some head has all 4 slots live and some has one.
All inputs are finite; a program needn't handle non-finite values.
Results may differ from the reference program's by a relative error of at most 0.0057.
Values may be sent and summed in bfloat16 or wider, within the bound.
A program may use at most 128 MiB of HBM per device.

```python
import math
import jax
import jax.numpy as jnp
from jax import lax

D = 16384
HEADS = 128
KVH = 8
HD = 128
OBLK = 128
OMAX = 4
ROWS = 8
SEQ = 512


def attention_pair(key):
    folded = jax.random.fold_in(key, 7)
    query_key, cache_key = jax.random.split(folded, 2)
    cache_drawn = jnp.clip(jax.random.normal(cache_key, (2, ROWS, SEQ, KVH * HD), jnp.float32), -4.0, 4.0)
    query_drawn = jnp.clip(jax.random.normal(query_key, (ROWS, HEADS * HD), jnp.float32), -4.0, 4.0)
    return (query_drawn, cache_drawn)


def draw_queries(key, part):
    return attention_pair(key)[0].astype(jnp.bfloat16)


def draw_kv_cache(key, part):
    return attention_pair(key)[1].astype(jnp.bfloat16)


def draw_lengths(key, part):
    folded = jax.random.fold_in(key, 11)
    key_one, key_two, key_three = jax.random.split(folded, 3)
    drawn = jax.random.randint(key_one, (ROWS,), 2, SEQ + 1, dtype=jnp.int32)
    first_row = jax.random.randint(key_two, (), 0, ROWS, dtype=jnp.int32)
    second_row = (first_row + 1 + jax.random.randint(key_three, (), 0, ROWS - 1, dtype=jnp.int32)) % ROWS
    return drawn.at[first_row].set(SEQ).at[second_row].set(2)


def draw_outlier_counts(key, part):
    folded = jax.random.fold_in(key, 13)
    key_one, key_two, key_three = jax.random.split(folded, 3)
    drawn = jax.random.randint(key_one, (HEADS,), 1, OMAX + 1, dtype=jnp.int32)
    first_head = jax.random.randint(key_two, (), 0, HEADS, dtype=jnp.int32)
    second_head = (first_head + 1 + jax.random.randint(key_three, (), 0, HEADS - 1, dtype=jnp.int32)) % HEADS
    return drawn.at[first_head].set(OMAX).at[second_head].set(1)


def touch_ends(values, stream_key, least, high):
    extent = values.shape
    place = [jax.random.randint(jax.random.fold_in(stream_key, axis), (), 0, extent[axis]) for axis in range(len(extent))]
    values = values.at[tuple(place)].set(least)
    longest = extent.index(max(extent))
    place[longest] = (place[longest] + 1) % extent[longest]
    return values.at[tuple(place)].set(high)


def with_spikes(entries, key, source, target, shards_of, factor):
    owner, partner = [(jnp.arange(entries.shape[position]) // (entries.shape[position] // shards_of)).reshape([-1 if axis == position else 1 for axis in range(entries.ndim)]) for position in (source, target)]
    chosen = jax.random.permutation(key, shards_of)[partner]
    strong = (owner == chosen) | (owner == (partner + shards_of // 2) % shards_of)
    return jnp.where(strong, factor * entries, entries)


def shard_levels(rng, dims, pieces, least, top_value):
    level = 1.0
    for axis_at, parts in pieces:
        steps = jax.random.uniform(jax.random.fold_in(jax.random.fold_in(rng, 6), axis_at), (parts,), jnp.float32, least / len(pieces), top_value / len(pieces))
        level = level * jnp.repeat(jnp.exp(steps), dims[axis_at] // parts).reshape((-1,) + (1,) * (len(dims) - 1 - axis_at))
    return level


def scatter_about(stream_key, extent, spread, reach, cuts=(), kind=jnp.bfloat16):
    gain = shard_levels(stream_key, extent, cuts, -0.22, 0.18) if cuts else 1.0
    values = jax.random.normal(stream_key, extent, jnp.float32) * spread * gain
    return jnp.minimum(jnp.maximum(values, -reach), reach).astype(kind)


def heavy_noise(own_key, dims, deviation, limit, shards, heavy, held_as=jnp.bfloat16):
    array = deviation * jax.random.normal(own_key, dims, jnp.float32)
    if shards:
        array = array * shard_levels(own_key, dims, shards, -0.22, 0.18)
    return jnp.clip(with_spikes(array, jax.random.fold_in(own_key, 3), *heavy), -limit, limit).astype(held_as)


def setup_inputs(seed: int = 0, part: int = 0) -> dict:
    arg_keys = jax.random.split(jax.random.key(seed), 8)
    part_keys = jax.random.split(jax.random.fold_in(arg_keys[7], part), 8)
    return {
        "queries": draw_queries(jax.random.fold_in(jax.random.fold_in(arg_keys[7], part), 71), part),
        "kv_cache": draw_kv_cache(jax.random.fold_in(jax.random.fold_in(arg_keys[7], part), 71), part),
        "lengths": draw_lengths(jax.random.fold_in(jax.random.fold_in(arg_keys[7], part), 71), part),
        "out_weight": heavy_noise(arg_keys[3], (HEADS * HD, D), 0.15, 0.8984375, ((0, 16),), (0, 1, 16, 2.0)),
        "outlier_values": scatter_about(arg_keys[4], (HEADS, OMAX, HD, OBLK), 0.5, 3.0, ((0, 16),)),
        "outlier_columns": touch_ends(jax.random.randint(arg_keys[5], (HEADS, OMAX), 0, D // OBLK), jax.random.fold_in(arg_keys[5], 1), 0, (D // OBLK) - 1).astype(jnp.int32),
        "outlier_counts": draw_outlier_counts(jax.random.fold_in(arg_keys[7], 71), part),
    }


def reference(queries, kv_cache, lengths, out_weight, outlier_values, outlier_columns, outlier_counts):
    row_count = queries.shape[0]
    group_size = HEADS // KVH
    key_rows = kv_cache[0].reshape(row_count, SEQ, KVH, HD).astype(jnp.float32)
    value_rows = kv_cache[1].reshape(row_count, SEQ, KVH, HD).astype(jnp.float32)
    queried = queries.reshape(row_count, KVH, group_size, HD).astype(jnp.float32)
    scores = jnp.einsum('rkgd,rskd->rkgs', queried, key_rows) / math.sqrt(HD)
    visible = jnp.arange(SEQ, dtype=jnp.int32)[None, :] < lengths[:, None]
    scores = jnp.where(visible[:, None, None, :], scores, -1e+30)
    row_peak = lax.optimization_barrier(jnp.max(scores, axis=-1, keepdims=True))
    raised = jnp.exp(scores - row_peak)
    totals = lax.optimization_barrier(jnp.sum(raised, axis=-1, keepdims=True))
    weights = (raised / totals).astype(jnp.bfloat16)
    attended = jnp.einsum('rkgs,rskd->rkgd', weights.astype(jnp.float32), value_rows)
    attended = attended.reshape(row_count, HEADS * HD).astype(jnp.bfloat16)
    projected = jnp.dot(attended, out_weight, preferred_element_type=jnp.float32)
    heads_attended = attended.reshape(row_count, HEADS, HD).astype(jnp.float32)
    slot_live = jnp.arange(OMAX, dtype=jnp.int32)[None, :] < outlier_counts[:, None]
    outlier_terms = jnp.einsum('rhd,hodc->rhoc', heads_attended, outlier_values.astype(jnp.float32))
    placement = ((outlier_columns[:, :, None] == jnp.arange(D // OBLK, dtype=jnp.int32)[None, None, :]) & slot_live[:, :, None]).astype(jnp.float32)
    correction = jnp.einsum('rhoc,hob->rbc', outlier_terms, placement).reshape(row_count, D)
    return (projected + correction).astype(jnp.bfloat16)
```

```python
import functools
import math

import jax
import jax.numpy as jnp
from jax import lax
from jax.experimental import pallas as pl
from jax.experimental.pallas import tpu as pltpu
from jax.sharding import PartitionSpec as P

KVH = 8
HD = 128
AHEAD = 2
MESH = pl.DeviceIdType.MESH
F32 = jnp.float32
BF16 = jnp.bfloat16


def steps_of(index, n):
    steps, bit = [], 1
    while bit < n:
        steps.append(bit - 2 * bit * ((index // bit) % 2))
        bit *= 2
    return steps


def flip(index, steps, mask):
    for k, step in enumerate(steps):
        if (mask >> k) & 1:
            index = index + step
    return index


def kernel(
    n,
    q_hbm, kv_hbm, w_hbm, ov_hbm, len_hbm, col_hbm, cnt_hbm,
    out_ref,
    len_ref, col_ref, cnt_ref, qbuf, qown, kvown, kvbuf, wbuf, ovbuf, bias, osend, obuf, sstat, rstat, tbuf, place, cbuf,
    psend, precv, sbuf, rbuf,
    small_sem, kv_sem, kvs_sem, kvr_sem, qo_sem, qs_sem, qr_sem, w_sem, ov_sem, os_sem, or_sem, ts_sem, tr_sem,
    ps_sem, pr_sem, ss_sem, sr_sem,
):
    me = lax.axis_index("tensor")
    core = me % 2
    chip = me // 2
    partner = me + 1 - 2 * core
    chips = n // 2
    half = me // chips
    rows, width = q_hbm.shape
    hl = width // HD
    nr = hl * rows
    g = n // KVH
    kh = KVH // 2
    positions = kv_hbm.shape[2]
    cols = w_hbm.shape[1] // n
    omax = ov_hbm.shape[1]
    jb = cols // HD
    hw = kh * HD
    kvcols = rows * positions
    terms = hl * omax
    nblocks = n * jb
    my_slot = me - half * chips
    dev_steps = steps_of(me, n)
    chip_steps = steps_of(chip, chips)

    barrier = pltpu.get_barrier_semaphore()
    for i in range(n - 1, 0, -1):
        pl.semaphore_signal(barrier, inc=1, device_id={"tensor": flip(me, dev_steps, i)}, device_id_type=MESH)

    def far(i):
        return flip(chip, chip_steps, chips - 1 - i)

    def dest_of(i):
        return 2 * far(i // 2) + (core + 1 + i % 2) % 2

    q_stage = pltpu.make_async_copy(q_hbm, qown, qo_sem)
    q_stage.start()
    kv_own = pltpu.make_async_copy(kv_hbm, kvown, kv_sem)
    kv_own.start()
    small = [
        pltpu.make_async_copy(src, dst, small_sem.at[i])
        for i, (src, dst) in enumerate(((len_hbm, len_ref), (col_hbm, col_ref), (cnt_hbm, cnt_ref)))
    ]
    for copy in small:
        copy.start()

    swap = pltpu.make_async_remote_copy(
        src_ref=kvown.at[:, :, :, pl.ds(pl.multiple_of((1 - core) * hw, hw), hw)], dst_ref=kvbuf, send_sem=kvs_sem, recv_sem=kvr_sem,
        device_id={"tensor": partner}, device_id_type=MESH,
    )

    def q_send(i):
        target = 2 * far(i) + half
        return target, pltpu.make_async_remote_copy(
            src_ref=qown, dst_ref=qbuf.at[my_slot], send_sem=qs_sem.at[i], recv_sem=qr_sem.at[my_slot],
            device_id={"tensor": target}, device_id_type=MESH,
        )

    def w_copy(i):
        return pltpu.make_async_copy(
            w_hbm.at[:, pl.ds(pl.multiple_of(dest_of(i) * cols, cols), cols)], wbuf.at[i], w_sem.at[i]
        )

    ov_copy = pltpu.make_async_copy(ov_hbm, ovbuf, ov_sem)

    @pl.when(me < n)
    def _():
        ov_copy.start()
        for i in range(n):
            w_copy(i).start()

    with jax.named_scope("barrier"):
        q_stage.wait()
        pl.semaphore_wait(barrier, n - 1)

    for i in range(chips):
        target, copy = q_send(i)
        if i < chips - 1:
            copy.start()
        else:
            pl.when(target != me)(copy.start)

    kv_own.wait()
    swap.start()

    @pl.when(half == core)
    def _():
        pltpu.make_async_copy(qown, qbuf.at[my_slot], qr_sem.at[my_slot]).start()

    with jax.named_scope("masks"):
        for copy in small:
            copy.wait()
        rowreq = lax.broadcasted_iota(jnp.int32, (g * nr, kvcols), 0) % rows
        colidx = lax.broadcasted_iota(jnp.int32, (1, kvcols), 1)
        colreq = colidx // positions
        limit = jnp.zeros((1, kvcols), jnp.int32)
        for r in range(rows):
            limit = jnp.where(colreq == r, len_ref[r], limit)
        for part in range(2):
            dev = me if part == 0 else partner
            live = (colidx % positions + dev * positions) < limit
            tag = jnp.where(live, colreq, -1)
            bias[part] = jnp.where(rowreq == tag, 0.0, -1e30).astype(F32)
        lane = lax.broadcasted_iota(jnp.int32, (nblocks, 2 * terms), 1) % terms
        row = lax.broadcasted_iota(jnp.int32, (nblocks, 2 * terms), 0)
        wanted = jnp.full((nblocks, 2 * terms), -1, jnp.int32)
        for h in range(hl):
            for o in range(omax):
                wanted = jnp.where(lane == h * omax + o, jnp.where(o < cnt_ref[h], col_ref[o, h], -1), wanted)
        place[...] = jnp.where(wanted == row, 1.0, 0.0).astype(BF16)

    with jax.named_scope("kvwait"):
        swap.wait()

    eye = lax.broadcasted_iota(jnp.int32, (g * nr, HD), 0) == lax.broadcasted_iota(jnp.int32, (g * nr, HD), 1)

    def to_row(column):
        return jnp.sum(jnp.where(eye, column, 0.0), axis=0, keepdims=True)

    def o_send(j):
        target = core * chips + j
        return target, pltpu.make_async_remote_copy(
            src_ref=osend.at[j], dst_ref=obuf.at[chip], send_sem=os_sem.at[j], recv_sem=or_sem.at[chip],
            device_id={"tensor": target}, device_id_type=MESH,
        )

    def t_send(j):
        return pltpu.make_async_remote_copy(
            src_ref=sstat.at[j], dst_ref=rstat.at[chip], send_sem=ts_sem.at[j], recv_sem=tr_sem.at[chip],
            device_id={"tensor": core * chips + j}, device_id_type=MESH,
        )

    def send_or_keep(j, remote, src, dst, sem):
        target = core * chips + j

        @pl.when(target != me)
        def _():
            remote.start()

        @pl.when(target == me)
        def _():
            pltpu.make_async_copy(src.at[j], dst.at[chip], sem.at[chip]).start()

    kl_here = (chip * 2 // g) % kh
    kl_steps = steps_of(kl_here, kh)
    with jax.named_scope("attention"):
        for step in range(kh):
            kl = flip(kl_here, kl_steps, kh - 1 - step)
            lanes = pl.ds(pl.multiple_of(kl * HD, HD), HD)
            own_lanes = pl.ds(pl.multiple_of(core * hw + kl * HD, HD), HD)
            pieces = []
            with jax.named_scope("qw%d" % step):
                for dl in range(g):
                    slot = kl * g + dl
                    pltpu.make_async_copy(qbuf.at[slot], qbuf.at[slot], qr_sem.at[slot]).wait()
            for dl in range(g):
                got = qbuf[kl * g + dl].astype(F32)
                pieces += [got[:, h * HD:(h + 1) * HD] for h in range(hl)]
            q = jnp.concatenate(pieces, axis=0).astype(BF16)
            scores, values = [], []
            for part in range(2):
                held, at = (kvown, own_lanes) if part == 0 else (kvbuf, lanes)
                keys = held[0, :, :, at].reshape(kvcols, HD)
                values.append(held[1, :, :, at].reshape(kvcols, HD))
                s = lax.dot_general(q, keys, (((1,), (1,)), ((), ())), preferred_element_type=F32)
                scores.append(s * (1.0 / math.sqrt(HD)) + bias[part])
            peak = jnp.maximum(
                jnp.max(scores[0], axis=-1, keepdims=True), jnp.max(scores[1], axis=-1, keepdims=True)
            )
            peak = jnp.maximum(peak, -(2.0**66))
            total = jnp.zeros((g * nr, 1), F32)
            o = jnp.zeros((g * nr, HD), F32)
            for part in range(2):
                raised = jnp.exp(scores[part] - peak)
                total = total + jnp.sum(raised, axis=-1, keepdims=True)
                o = o + jnp.dot(raised.astype(BF16), values[part], preferred_element_type=F32)
            stats = jnp.concatenate([to_row(peak), to_row(total)], axis=0)
            o = o.astype(BF16)
            for dl in range(g):
                slot = kl * g + dl
                sstat[slot] = stats
                osend[slot] = o[dl * nr:(dl + 1) * nr]
            for dl in range(g):
                slot = kl * g + dl
                send_or_keep(slot, t_send(slot), sstat, rstat, tr_sem)
                send_or_keep(slot, o_send(slot)[1], osend, obuf, or_sem)

    with jax.named_scope("twait"):
        for p in range(chips):
            pltpu.make_async_copy(rstat.at[p], rstat.at[p], tr_sem.at[p]).wait()
    peaks = [rstat[p, 0:1, :] for p in range(chips)]
    totals = [rstat[p, 1:2, :] for p in range(chips)]
    peak = functools.reduce(jnp.maximum, peaks)
    shares = [jnp.exp(m - peak) for m in peaks]
    total = sum(s * t for s, t in zip(shares, totals))
    first = (me % g) * nr
    mine = (
        lax.broadcasted_iota(jnp.int32, (nr, HD), 0) + first
        == lax.broadcasted_iota(jnp.int32, (nr, HD), 1)
    )
    shares = [jnp.sum(jnp.where(mine, s / total, 0.0), axis=1, keepdims=True) for s in shares]
    with jax.named_scope("owait"):
        for p in range(chips):
            pltpu.make_async_copy(obuf.at[p], obuf.at[p], or_sem.at[p]).wait()
    with jax.named_scope("wwait"):
        ov_copy.wait()
        for i in range(n):
            w_copy(i).wait()

    with jax.named_scope("project"):
        attended = jnp.zeros((nr, HD), F32)
        for p in range(chips):
            attended = attended + shares[p] * obuf[p].astype(F32)
        a = jnp.concatenate([attended[h * rows:(h + 1) * rows] for h in range(hl)], axis=1).astype(BF16)

        for h in range(hl):
            for o in range(omax):
                t = h * omax + o
                tbuf[t * rows:(t + 1) * rows, :] = jnp.dot(
                    a[:, h * HD:(h + 1) * HD], ovbuf[h, o], preferred_element_type=F32
                )
        pieces = []
        for r in range(rows):
            term = tbuf[pl.ds(r, terms, stride=rows), :]
            high = term.astype(BF16)
            low = (term - high.astype(F32)).astype(BF16)
            pieces.append(jnp.concatenate([high, low], axis=0))
        placed = jnp.dot(place[...], jnp.concatenate(pieces, axis=1), preferred_element_type=F32)
        for r in range(rows):
            cbuf[r * nblocks:(r + 1) * nblocks, :] = placed[:, r * HD:(r + 1) * HD]

        def block(i):
            part = jnp.dot(a, wbuf[i], preferred_element_type=F32)
            first_block = dest_of(i) * jb
            return jnp.concatenate(
                [
                    part[:, j * HD:(j + 1) * HD] + cbuf[pl.ds(first_block + j, rows, stride=nblocks), :]
                    for j in range(jb)
                ],
                axis=1,
            )

        def p_send(i):
            return pltpu.make_async_remote_copy(
                src_ref=psend.at[i], dst_ref=precv.at[i], send_sem=ps_sem.at[i], recv_sem=pr_sem.at[i],
                device_id={"tensor": partner}, device_id_type=MESH,
            )

        def s_send(i):
            return pltpu.make_async_remote_copy(
                src_ref=sbuf.at[i], dst_ref=rbuf.at[i], send_sem=ss_sem.at[i], recv_sem=sr_sem.at[i],
                device_id={"tensor": 2 * far(i) + core}, device_id_type=MESH,
            )

        acc = None
        for k in range(0, chips + AHEAD, 1):
            j = k - AHEAD
            given = block(2 * k) if k < chips else None
            sums = block(2 * j + 1) if j >= 0 else None
            if given is not None:
                psend[k] = given
                p_send(k).start()
            if sums is not None:
                with jax.named_scope("pw%d" % j):
                    p_send(j).wait_recv()
                sums = sums + precv[j]
                if j < chips - 1:
                    sbuf[j] = sums.astype(BF16)
                    s_send(j).start()
                else:
                    acc = sums

    with jax.named_scope("gather"):
        swap_done = None
        for i in range(chips):
            target, copy = q_send(i)
            if i < chips - 1:
                copy.wait_send()
            else:
                pl.when(target != me)(copy.wait_send)
            target, copy = o_send(i)

            @pl.when(target != me)
            def _():
                copy.wait_send()
                t_send(i).wait_send()

            p_send(i).wait_send()
        for i in range(chips - 1):
            s_send(i).wait()
            acc = acc + rbuf[i].astype(F32)
        out_ref[...] = acc


def body(n, queries, kv_cache, lengths, out_weight, outlier_values, outlier_columns, outlier_counts):
    rows, width = queries.shape
    hl = width // HD
    nr = hl * rows
    positions = kv_cache.shape[2]
    cols = out_weight.shape[1] // n
    omax = outlier_values.shape[1]
    chips = n // 2
    g = n // KVH
    dma = pltpu.SemaphoreType.DMA
    out = pl.pallas_call(
        functools.partial(kernel, n),
        out_shape=jax.ShapeDtypeStruct((rows, cols), F32),
        in_specs=[pl.BlockSpec(memory_space=pl.ANY)] * 7,
        out_specs=pl.BlockSpec(memory_space=pltpu.VMEM),
        scratch_shapes=[
            pltpu.SMEM(lengths.shape, jnp.int32),
            pltpu.SMEM((omax, hl), jnp.int32),
            pltpu.SMEM(outlier_counts.shape, jnp.int32),
            pltpu.VMEM((chips, rows, width), BF16),
            pltpu.VMEM((rows, width), BF16),
            pltpu.VMEM(kv_cache.shape, BF16),
            pltpu.VMEM((2, rows, positions, KVH // 2 * HD), BF16),
            pltpu.VMEM((n, width, cols), BF16),
            pltpu.VMEM(outlier_values.shape, BF16),
            pltpu.VMEM((2, g * nr, rows * positions), F32),
            pltpu.VMEM((chips, nr, HD), BF16),
            pltpu.VMEM((chips, nr, HD), BF16),
            pltpu.VMEM((chips, 2, HD), F32),
            pltpu.VMEM((chips, 2, HD), F32),
            pltpu.VMEM((hl * omax * rows, HD), F32),
            pltpu.VMEM((n * cols // HD, 2 * hl * omax), BF16),
            pltpu.VMEM((rows * (n * cols // HD), HD), F32),
            pltpu.VMEM((chips, rows, cols), F32),
            pltpu.VMEM((chips, rows, cols), F32),
            pltpu.VMEM((chips, rows, cols), BF16),
            pltpu.VMEM((chips, rows, cols), BF16),
            dma((3,)), dma, dma, dma, dma, dma((chips,)), dma((chips,)), dma((n,)), dma, dma((chips,)), dma((chips,)),
            dma((chips,)), dma((chips,)), dma((chips,)), dma((chips,)), dma((chips,)), dma((chips,)),
        ],
        compiler_params=pltpu.CompilerParams(
            collective_id=0, has_side_effects=True, vmem_limit_bytes=60 * 2**20
        ),
    )(queries, kv_cache, out_weight, outlier_values, lengths, outlier_columns.T, outlier_counts)
    return out.astype(BF16)


def solution(mesh):
    placed = (
        P("groups", "tensor"),
        P(None, "groups", "tensor", None),
        P("groups"),
        P("tensor", None),
        P("tensor", None, None, None),
        P("tensor", None),
        P("tensor"),
    )
    return jax.shard_map(
        functools.partial(body, mesh.shape["tensor"]),
        mesh=mesh, in_specs=placed, out_specs=P("groups", "tensor"), check_vma=False,
    )
```

```python
import functools
import math

import jax
import jax.numpy as jnp
from jax import lax
from jax.experimental import pallas as pl
from jax.experimental.pallas import tpu as pltpu
from jax.sharding import PartitionSpec as P

KVH = 8
HD = 128
MESH = pl.DeviceIdType.MESH
F32 = jnp.float32
BF16 = jnp.bfloat16


def steps_of(index, n):
    steps, bit = [], 1
    while bit < n:
        steps.append(bit - 2 * bit * ((index // bit) % 2))
        bit *= 2
    return steps


def flip(index, steps, mask):
    for k, step in enumerate(steps):
        if (mask >> k) & 1:
            index = index + step
    return index


def kernel(
    n,
    q_hbm, kv_hbm, w_hbm, ov_hbm, len_hbm, col_hbm, cnt_hbm,
    out_ref,
    len_ref, col_ref, cnt_ref, qbuf, qown, kvown, kvbuf, wbuf, ovbuf, bias, osend, obuf, sstat, rstat, tbuf, place, cbuf,
    psend, precv, sbuf, rbuf,
    small_sem, kv_sem, kvs_sem, kvr_sem, qo_sem, qs_sem, qr_sem, w_sem, ov_sem, os_sem, or_sem, ts_sem, tr_sem,
    ps_sem, pr_sem, ss_sem, sr_sem,
):
    me = lax.axis_index("tensor")
    core = me % 2
    chip = me // 2
    partner = me + 1 - 2 * core
    chips = n // 2
    half = me // chips
    rows, width = q_hbm.shape
    hl = width // HD
    nr = hl * rows
    g = n // KVH
    kh = KVH // 2
    positions = kv_hbm.shape[2]
    cols = w_hbm.shape[1] // n
    omax = ov_hbm.shape[1]
    jb = cols // HD
    hw = kh * HD
    kvcols = rows * positions
    terms = hl * omax
    nblocks = n * jb
    my_slot = me - half * chips
    dev_steps = steps_of(me, n)
    chip_steps = steps_of(chip, chips)

    barrier = pltpu.get_barrier_semaphore()
    for i in range(n - 1, 0, -1):
        pl.semaphore_signal(barrier, inc=1, device_id={"tensor": flip(me, dev_steps, i)}, device_id_type=MESH)

    def far(i):
        return flip(chip, chip_steps, chips - 1 - i)

    def dest_of(i):
        return 2 * far(i // 2) + (core + 1 + i % 2) % 2

    q_stage = pltpu.make_async_copy(q_hbm, qown, qo_sem)
    q_stage.start()
    kv_own = pltpu.make_async_copy(kv_hbm, kvown, kv_sem)
    kv_own.start()
    small = [
        pltpu.make_async_copy(src, dst, small_sem.at[i])
        for i, (src, dst) in enumerate(((len_hbm, len_ref), (col_hbm, col_ref), (cnt_hbm, cnt_ref)))
    ]
    for copy in small:
        copy.start()

    swap = pltpu.make_async_remote_copy(
        src_ref=kvown.at[:, :, :, pl.ds(pl.multiple_of((1 - core) * hw, hw), hw)], dst_ref=kvbuf, send_sem=kvs_sem, recv_sem=kvr_sem,
        device_id={"tensor": partner}, device_id_type=MESH,
    )

    def q_send(i):
        target = 2 * far(i) + half
        return target, pltpu.make_async_remote_copy(
            src_ref=qown, dst_ref=qbuf.at[my_slot], send_sem=qs_sem.at[i], recv_sem=qr_sem.at[my_slot],
            device_id={"tensor": target}, device_id_type=MESH,
        )

    def w_copy(i):
        return pltpu.make_async_copy(
            w_hbm.at[:, pl.ds(pl.multiple_of(dest_of(i) * cols, cols), cols)], wbuf.at[i], w_sem.at[i]
        )

    ov_copy = pltpu.make_async_copy(ov_hbm, ovbuf, ov_sem)

    @pl.when(me < n)
    def _():
        ov_copy.start()
        for i in range(n):
            w_copy(i).start()

    with jax.named_scope("barrier"):
        q_stage.wait()
        pl.semaphore_wait(barrier, n - 1)

    for i in range(chips):
        target, copy = q_send(i)
        if i < chips - 1:
            copy.start()
        else:
            pl.when(target != me)(copy.start)

    kv_own.wait()
    swap.start()

    @pl.when(half == core)
    def _():
        pltpu.make_async_copy(qown, qbuf.at[my_slot], qr_sem.at[my_slot]).start()

    with jax.named_scope("masks"):
        for copy in small:
            copy.wait()
        rowreq = lax.broadcasted_iota(jnp.int32, (g * nr, kvcols), 0) % rows
        colidx = lax.broadcasted_iota(jnp.int32, (1, kvcols), 1)
        colreq = colidx // positions
        limit = jnp.zeros((1, kvcols), jnp.int32)
        for r in range(rows):
            limit = jnp.where(colreq == r, len_ref[r], limit)
        for part in range(2):
            dev = me if part == 0 else partner
            live = (colidx % positions + dev * positions) < limit
            tag = jnp.where(live, colreq, -1)
            bias[part] = jnp.where(rowreq == tag, 0.0, -1e30).astype(F32)
        lane = lax.broadcasted_iota(jnp.int32, (nblocks, 2 * terms), 1) % terms
        row = lax.broadcasted_iota(jnp.int32, (nblocks, 2 * terms), 0)
        wanted = jnp.full((nblocks, 2 * terms), -1, jnp.int32)
        for h in range(hl):
            for o in range(omax):
                wanted = jnp.where(lane == h * omax + o, jnp.where(o < cnt_ref[h], col_ref[o, h], -1), wanted)
        place[...] = jnp.where(wanted == row, 1.0, 0.0).astype(BF16)

    with jax.named_scope("kvwait"):
        swap.wait()

    eye = lax.broadcasted_iota(jnp.int32, (g * nr, HD), 0) == lax.broadcasted_iota(jnp.int32, (g * nr, HD), 1)

    def to_row(column):
        return jnp.sum(jnp.where(eye, column, 0.0), axis=0, keepdims=True)

    def o_send(j):
        target = core * chips + j
        return target, pltpu.make_async_remote_copy(
            src_ref=osend.at[j], dst_ref=obuf.at[chip], send_sem=os_sem.at[j], recv_sem=or_sem.at[chip],
            device_id={"tensor": target}, device_id_type=MESH,
        )

    def t_send(j):
        return pltpu.make_async_remote_copy(
            src_ref=sstat.at[j], dst_ref=rstat.at[chip], send_sem=ts_sem.at[j], recv_sem=tr_sem.at[chip],
            device_id={"tensor": core * chips + j}, device_id_type=MESH,
        )

    def send_or_keep(j, remote, src, dst, sem):
        target = core * chips + j

        @pl.when(target != me)
        def _():
            remote.start()

        @pl.when(target == me)
        def _():
            pltpu.make_async_copy(src.at[j], dst.at[chip], sem.at[chip]).start()

    kl_here = (chip * 2 // g) % kh
    kl_steps = steps_of(kl_here, kh)
    def attend(kl):
        own_lanes = pl.ds(pl.multiple_of(core * hw + kl * HD, HD), HD)
        lanes = pl.ds(pl.multiple_of(kl * HD, HD), HD)
        pieces = []
        for dl in range(g):
            got = qbuf[kl * g + dl].astype(F32)
            pieces += [got[:, h * HD:(h + 1) * HD] for h in range(hl)]
        q = jnp.concatenate(pieces, axis=0).astype(BF16)
        scores, values = [], []
        for part in range(2):
            held, at = (kvown, own_lanes) if part == 0 else (kvbuf, lanes)
            keys = held[0, :, :, at].reshape(kvcols, HD)
            values.append(held[1, :, :, at].reshape(kvcols, HD))
            s = lax.dot_general(q, keys, (((1,), (1,)), ((), ())), preferred_element_type=F32)
            scores.append(s * (1.0 / math.sqrt(HD)) + bias[part])
        peak = jnp.max(jnp.maximum(scores[0], scores[1]), axis=-1, keepdims=True)
        peak = jnp.maximum(peak, -(2.0**66))
        raised = [jnp.exp(s - peak) for s in scores]
        total = jnp.sum(raised[0] + raised[1], axis=-1, keepdims=True)
        o = jnp.dot(raised[0].astype(BF16), values[0], preferred_element_type=F32)
        o = o + jnp.dot(raised[1].astype(BF16), values[1], preferred_element_type=F32)
        stats = jnp.concatenate([to_row(peak), to_row(total)], axis=0)
        return stats, o.astype(BF16)

    per = 1
    with jax.named_scope("attention"):
        for group in range(0, kh, per):
            kls = [flip(kl_here, kl_steps, kh - 1 - step) for step in range(group, group + per)]
            with jax.named_scope("qw%d" % group):
                for kl in kls:
                    for dl in range(g):
                        slot = kl * g + dl
                        pltpu.make_async_copy(qbuf.at[slot], qbuf.at[slot], qr_sem.at[slot]).wait()
            found = [attend(kl) for kl in kls]
            for kl, (stats, o) in zip(kls, found):
                for dl in range(g):
                    sstat[kl * g + dl] = stats
                    osend[kl * g + dl] = o[dl * nr:(dl + 1) * nr]
            for step, kl in zip(range(group, group + per), kls):
                for dl in range(g):
                    slot = kl * g + dl
                    if step < kh - 1:
                        t_send(slot).start()
                        o_send(slot)[1].start()
                    else:
                        send_or_keep(slot, t_send(slot), sstat, rstat, tr_sem)
                        send_or_keep(slot, o_send(slot)[1], osend, obuf, or_sem)

    with jax.named_scope("twait"):
        for p in range(chips):
            pltpu.make_async_copy(rstat.at[p], rstat.at[p], tr_sem.at[p]).wait()
    peaks = [rstat[p, 0:1, :] for p in range(chips)]
    totals = [rstat[p, 1:2, :] for p in range(chips)]
    peak = functools.reduce(jnp.maximum, peaks)
    shares = [jnp.exp(m - peak) for m in peaks]
    total = sum(s * t for s, t in zip(shares, totals))
    first = (me % g) * nr
    mine = (
        lax.broadcasted_iota(jnp.int32, (nr, HD), 0) + first
        == lax.broadcasted_iota(jnp.int32, (nr, HD), 1)
    )
    shares = [jnp.sum(jnp.where(mine, s / total, 0.0), axis=1, keepdims=True) for s in shares]
    with jax.named_scope("owait"):
        for p in range(chips):
            pltpu.make_async_copy(obuf.at[p], obuf.at[p], or_sem.at[p]).wait()
    with jax.named_scope("wwait"):
        ov_copy.wait()
        for i in range(n):
            w_copy(i).wait()

    with jax.named_scope("project"):
        attended = jnp.zeros((nr, HD), F32)
        for p in range(chips):
            attended = attended + shares[p] * obuf[p].astype(F32)
        a = jnp.concatenate([attended[h * rows:(h + 1) * rows] for h in range(hl)], axis=1).astype(BF16)

        def correct(i, part):
            first_block = dest_of(i) * jb
            return jnp.concatenate(
                [
                    part[:, j * HD:(j + 1) * HD] + cbuf[pl.ds(first_block + j, rows, stride=nblocks), :]
                    for j in range(jb)
                ],
                axis=1,
            )

        def p_send(i):
            return pltpu.make_async_remote_copy(
                src_ref=psend.at[i], dst_ref=precv.at[i], send_sem=ps_sem.at[i], recv_sem=pr_sem.at[i],
                device_id={"tensor": partner}, device_id_type=MESH,
            )

        def s_send(i):
            return pltpu.make_async_remote_copy(
                src_ref=sbuf.at[i], dst_ref=rbuf.at[i], send_sem=ss_sem.at[i], recv_sem=sr_sem.at[i],
                device_id={"tensor": 2 * far(i) + core}, device_id_type=MESH,
            )

        acc = None
        cross = chips // 2
        groups = [[(0, k), (0, k + 1)] for k in range(0, cross, 2)]
        groups += [[(1, k), (1, k + 1)] for k in range(0, cross, 2)]
        groups += [[(0, k) for k in range(cross, chips - 1)]]
        groups += [[(1, k) for k in range(cross, chips - 2)] + [(0, chips - 1)]]
        groups += [[(1, chips - 2)], [(1, chips - 1)]]
        for turn, group in enumerate(groups):
            if turn == 0:
                for h in range(hl):
                    for o in range(omax):
                        t = h * omax + o
                        tbuf[t * rows:(t + 1) * rows, :] = jnp.dot(
                            a[:, h * HD:(h + 1) * HD], ovbuf[h, o], preferred_element_type=F32
                        )
                pieces = []
                for r in range(rows):
                    term = tbuf[pl.ds(r, terms, stride=rows), :]
                    high = term.astype(BF16)
                    low = (term - high.astype(F32)).astype(BF16)
                    pieces.append(jnp.concatenate([high, low], axis=0))
                placed = jnp.dot(place[...], jnp.concatenate(pieces, axis=1), preferred_element_type=F32)
                for r in range(rows):
                    cbuf[r * nblocks:(r + 1) * nblocks, :] = placed[:, r * HD:(r + 1) * HD]
            parts = [jnp.dot(a, wbuf[2 * k + keep], preferred_element_type=F32) for keep, k in group]
            parts = [correct(2 * k + keep, part) for (keep, k), part in zip(group, parts)]
            for (keep, k), part in zip(group, parts):
                if not keep:
                    psend[k] = part
            for keep, k in group:
                if not keep:
                    p_send(k).start()
            for (keep, k), part in zip(group, parts):
                if keep:
                    with jax.named_scope("pw%d" % k):
                        p_send(k).wait_recv()
                    part = part + precv[k]
                    if k < chips - 1:
                        sbuf[k] = part.astype(BF16)
                        s_send(k).start()
                    else:
                        acc = part

    with jax.named_scope("gather"):
        for i in range(chips):
            target, copy = q_send(i)
            if i < chips - 1:
                copy.wait_send()
            else:
                pl.when(target != me)(copy.wait_send)
            target, copy = o_send(i)

            @pl.when(target != me)
            def _():
                copy.wait_send()
                t_send(i).wait_send()

            p_send(i).wait_send()
        for i in range(chips - 1):
            s_send(i).wait()
            acc = acc + rbuf[i].astype(F32)
        out_ref[...] = acc.astype(BF16)


def body(n, queries, kv_cache, lengths, out_weight, outlier_values, outlier_columns, outlier_counts):
    rows, width = queries.shape
    hl = width // HD
    nr = hl * rows
    positions = kv_cache.shape[2]
    cols = out_weight.shape[1] // n
    omax = outlier_values.shape[1]
    chips = n // 2
    g = n // KVH
    dma = pltpu.SemaphoreType.DMA
    out = pl.pallas_call(
        functools.partial(kernel, n),
        out_shape=pltpu.VMEM((rows, cols), BF16),
        in_specs=[pl.BlockSpec(memory_space=pl.ANY)] * 7,
        out_specs=pl.BlockSpec(memory_space=pltpu.VMEM),
        scratch_shapes=[
            pltpu.SMEM(lengths.shape, jnp.int32),
            pltpu.SMEM((omax, hl), jnp.int32),
            pltpu.SMEM(outlier_counts.shape, jnp.int32),
            pltpu.VMEM((chips, rows, width), BF16),
            pltpu.VMEM((rows, width), BF16),
            pltpu.VMEM(kv_cache.shape, BF16),
            pltpu.VMEM((2, rows, positions, KVH // 2 * HD), BF16),
            pltpu.VMEM((n, width, cols), BF16),
            pltpu.VMEM(outlier_values.shape, BF16),
            pltpu.VMEM((2, g * nr, rows * positions), F32),
            pltpu.VMEM((chips, nr, HD), BF16),
            pltpu.VMEM((chips, nr, HD), BF16),
            pltpu.VMEM((chips, 2, HD), F32),
            pltpu.VMEM((chips, 2, HD), F32),
            pltpu.VMEM((hl * omax * rows, HD), F32),
            pltpu.VMEM((n * cols // HD, 2 * hl * omax), BF16),
            pltpu.VMEM((rows * (n * cols // HD), HD), F32),
            pltpu.VMEM((chips, rows, cols), F32),
            pltpu.VMEM((chips, rows, cols), F32),
            pltpu.VMEM((chips, rows, cols), BF16),
            pltpu.VMEM((chips, rows, cols), BF16),
            dma((3,)), dma, dma, dma, dma, dma((chips,)), dma((chips,)), dma((n,)), dma, dma((chips,)), dma((chips,)),
            dma((chips,)), dma((chips,)), dma((chips,)), dma((chips,)), dma((chips,)), dma((chips,)),
        ],
        compiler_params=pltpu.CompilerParams(
            collective_id=0, has_side_effects=True, vmem_limit_bytes=56 * 2**20
        ),
    )(queries, kv_cache, out_weight, outlier_values, lengths, outlier_columns.T, outlier_counts)
    return out


def solution(mesh):
    placed = (
        P("groups", "tensor"),
        P(None, "groups", "tensor", None),
        P("groups"),
        P("tensor", None),
        P("tensor", None, None, None),
        P("tensor", None),
        P("tensor"),
    )
    return jax.shard_map(
        functools.partial(body, mesh.shape["tensor"]),
        mesh=mesh, in_specs=placed, out_specs=P("groups", "tensor"), check_vma=False,
    )
```

```python
import functools
import math

import jax
import jax.numpy as jnp
from jax import lax
from jax.experimental import pallas as pl
from jax.experimental.pallas import tpu as pltpu
from jax.sharding import PartitionSpec as P

KVH = 8
HD = 128
MESH = pl.DeviceIdType.MESH
F32 = jnp.float32
BF16 = jnp.bfloat16


def steps_of(index, n):
    steps, bit = [], 1
    while bit < n:
        steps.append(bit - 2 * bit * ((index // bit) % 2))
        bit *= 2
    return steps


def flip(index, steps, mask):
    for k, step in enumerate(steps):
        if (mask >> k) & 1:
            index = index + step
    return index


def kernel(
    n,
    q_hbm, kv_hbm, w_hbm, ov_hbm, len_hbm, col_hbm, cnt_hbm,
    out_ref,
    len_ref, col_ref, cnt_ref, qbuf, qown, kvown, kvbuf, wbuf, ovbuf, bias, turned, osend, obuf, sstat, rstat, tbuf, place, cbuf,
    psend, precv, sbuf, rbuf,
    small_sem, kv_sem, kvs_sem, kvr_sem, qo_sem, qs_sem, qr_sem, w_sem, ov_sem, os_sem, or_sem, ts_sem, tr_sem,
    ps_sem, pr_sem, ss_sem, sr_sem,
):
    me = lax.axis_index("tensor")
    core = me % 2
    chip = me // 2
    partner = me + 1 - 2 * core
    chips = n // 2
    half = me // chips
    rows, width = q_hbm.shape
    hl = width // HD
    nr = hl * rows
    g = n // KVH
    kh = KVH // 2
    positions = kv_hbm.shape[2]
    cols = w_hbm.shape[1] // n
    omax = ov_hbm.shape[1]
    jb = cols // HD
    hw = kh * HD
    kvcols = rows * positions
    terms = hl * omax
    nblocks = n * jb
    my_slot = me - half * chips
    dev_steps = steps_of(me, n)
    chip_steps = steps_of(chip, chips)

    barrier = pltpu.get_barrier_semaphore()
    for i in range(n - 1, 0, -1):
        pl.semaphore_signal(barrier, inc=1, device_id={"tensor": flip(me, dev_steps, i)}, device_id_type=MESH)

    def far(i):
        return flip(chip, chip_steps, chips - 1 - i)

    def dest_of(i):
        return 2 * far(i // 2) + (core + 1 + i % 2) % 2

    q_stage = pltpu.make_async_copy(q_hbm, qown, qo_sem)
    q_stage.start()
    kv_own = pltpu.make_async_copy(kv_hbm, kvown, kv_sem)
    kv_own.start()
    small = [
        pltpu.make_async_copy(src, dst, small_sem.at[i])
        for i, (src, dst) in enumerate(((len_hbm, len_ref), (col_hbm, col_ref), (cnt_hbm, cnt_ref)))
    ]
    for copy in small:
        copy.start()

    swap = pltpu.make_async_remote_copy(
        src_ref=kvown.at[:, :, :, pl.ds(pl.multiple_of((1 - core) * hw, hw), hw)], dst_ref=kvbuf, send_sem=kvs_sem, recv_sem=kvr_sem,
        device_id={"tensor": partner}, device_id_type=MESH,
    )

    def q_send(i):
        target = 2 * far(i) + half
        return target, pltpu.make_async_remote_copy(
            src_ref=qown, dst_ref=qbuf.at[my_slot], send_sem=qs_sem.at[i], recv_sem=qr_sem.at[my_slot],
            device_id={"tensor": target}, device_id_type=MESH,
        )

    def w_copy(i):
        return pltpu.make_async_copy(
            w_hbm.at[:, pl.ds(pl.multiple_of(dest_of(i) * cols, cols), cols)], wbuf.at[i], w_sem.at[i]
        )

    ov_copy = pltpu.make_async_copy(ov_hbm, ovbuf, ov_sem)

    @pl.when(me < n)
    def _():
        ov_copy.start()
        for i in range(n):
            w_copy(i).start()

    with jax.named_scope("barrier"):
        q_stage.wait()
        pl.semaphore_wait(barrier, n - 1)

    apart = chips // 2
    window = 3

    def q_start(i):
        target, copy = q_send(i)
        if i < chips - 1:
            copy.start()
        else:
            pl.when(target != me)(copy.start)

    for i in range(window):
        q_start(i)
    kv_own.wait()
    swap.start()

    @pl.when(half == core)
    def _():
        pltpu.make_async_copy(qown, qbuf.at[my_slot], qr_sem.at[my_slot]).start()

    with jax.named_scope("pace"):
        for i in range(window, apart):
            q_send(i - window)[1].wait_send()
            q_start(i)
        for i in range(apart, chips):
            q_start(i)

    with jax.named_scope("masks"):
        for copy in small:
            copy.wait()
        rowreq = lax.broadcasted_iota(jnp.int32, (g * nr, kvcols), 0) % rows
        colidx = lax.broadcasted_iota(jnp.int32, (1, kvcols), 1)
        colreq = colidx // positions
        limit = jnp.zeros((1, kvcols), jnp.int32)
        for r in range(rows):
            limit = jnp.where(colreq == r, len_ref[r], limit)
        for part in range(2):
            dev = me if part == 0 else partner
            live = (colidx % positions + dev * positions) < limit
            tag = jnp.where(live, colreq, -1)
            bias[part] = jnp.where(rowreq == tag, 0.0, -1e30).astype(F32)
        lane = lax.broadcasted_iota(jnp.int32, (nblocks, 2 * terms), 1) % terms
        row = lax.broadcasted_iota(jnp.int32, (nblocks, 2 * terms), 0)
        wanted = jnp.full((nblocks, 2 * terms), -1, jnp.int32)
        for h in range(hl):
            for o in range(omax):
                wanted = jnp.where(lane == h * omax + o, jnp.where(o < cnt_ref[h], col_ref[o, h], -1), wanted)
        place[...] = jnp.where(wanted == row, 1.0, 0.0).astype(BF16)

    with jax.named_scope("turn"):
        for kl in range(kh):
            own_lanes = pl.ds(pl.multiple_of(core * hw + kl * HD, HD), HD)
            turned[0, kl] = kvown[0, :, :, own_lanes].reshape(kvcols, HD).T
    with jax.named_scope("kvwait"):
        swap.wait()
    with jax.named_scope("turn2"):
        for kl in range(kh):
            turned[1, kl] = kvbuf[0, :, :, pl.ds(kl * HD, HD)].reshape(kvcols, HD).T

    eye = lax.broadcasted_iota(jnp.int32, (g * nr, HD), 0) == lax.broadcasted_iota(jnp.int32, (g * nr, HD), 1)

    def to_row(column):
        return jnp.sum(jnp.where(eye, column, 0.0), axis=0, keepdims=True)

    def o_send(j):
        target = core * chips + j
        return target, pltpu.make_async_remote_copy(
            src_ref=osend.at[j], dst_ref=obuf.at[chip], send_sem=os_sem.at[j], recv_sem=or_sem.at[chip],
            device_id={"tensor": target}, device_id_type=MESH,
        )

    def t_send(j):
        return pltpu.make_async_remote_copy(
            src_ref=sstat.at[j], dst_ref=rstat.at[chip], send_sem=ts_sem.at[j], recv_sem=tr_sem.at[chip],
            device_id={"tensor": core * chips + j}, device_id_type=MESH,
        )

    def send_or_keep(j, remote, src, dst, sem):
        target = core * chips + j

        @pl.when(target != me)
        def _():
            remote.start()

        @pl.when(target == me)
        def _():
            pltpu.make_async_copy(src.at[j], dst.at[chip], sem.at[chip]).start()

    kl_here = (chip * 2 // g) % kh
    kl_steps = steps_of(kl_here, kh)
    def attend(kl):
        own_lanes = pl.ds(pl.multiple_of(core * hw + kl * HD, HD), HD)
        lanes = pl.ds(pl.multiple_of(kl * HD, HD), HD)
        pieces = []
        for dl in range(g):
            got = qbuf[kl * g + dl].astype(F32)
            pieces += [got[:, h * HD:(h + 1) * HD] for h in range(hl)]
        q = jnp.concatenate(pieces, axis=0).astype(BF16)
        scores, values = [], []
        for part in range(2):
            held, at = (kvown, own_lanes) if part == 0 else (kvbuf, lanes)
            values.append(held[1, :, :, at].reshape(kvcols, HD))
            s = jnp.dot(q, turned[part, kl], preferred_element_type=F32)
            scores.append(s * (1.0 / math.sqrt(HD)) + bias[part])
        peak = jnp.max(jnp.maximum(scores[0], scores[1]), axis=-1, keepdims=True)
        peak = jnp.maximum(peak, -(2.0**66))
        raised = [jnp.exp(s - peak) for s in scores]
        total = jnp.sum(raised[0] + raised[1], axis=-1, keepdims=True)
        o = jnp.dot(raised[0].astype(BF16), values[0], preferred_element_type=F32)
        o = o + jnp.dot(raised[1].astype(BF16), values[1], preferred_element_type=F32)
        stats = jnp.concatenate([to_row(peak), to_row(total)], axis=0)
        return stats, o.astype(BF16)

    per = 1
    with jax.named_scope("attention"):
        for group in range(0, kh, per):
            kls = [flip(kl_here, kl_steps, kh - 1 - step) for step in range(group, group + per)]
            with jax.named_scope("qw%d" % group):
                for kl in kls:
                    for dl in range(g):
                        slot = kl * g + dl
                        pltpu.make_async_copy(qbuf.at[slot], qbuf.at[slot], qr_sem.at[slot]).wait()
            found = [attend(kl) for kl in kls]
            for kl, (stats, o) in zip(kls, found):
                for dl in range(g):
                    sstat[kl * g + dl] = stats
                    osend[kl * g + dl] = o[dl * nr:(dl + 1) * nr]
            for step, kl in zip(range(group, group + per), kls):
                for dl in range(g):
                    slot = kl * g + dl
                    if step < kh - 1:
                        t_send(slot).start()
                        o_send(slot)[1].start()
                    else:
                        send_or_keep(slot, t_send(slot), sstat, rstat, tr_sem)
                        send_or_keep(slot, o_send(slot)[1], osend, obuf, or_sem)

    with jax.named_scope("twait"):
        for p in range(chips):
            pltpu.make_async_copy(rstat.at[p], rstat.at[p], tr_sem.at[p]).wait()
    peaks = [rstat[p, 0:1, :] for p in range(chips)]
    totals = [rstat[p, 1:2, :] for p in range(chips)]
    peak = functools.reduce(jnp.maximum, peaks)
    shares = [jnp.exp(m - peak) for m in peaks]
    total = sum(s * t for s, t in zip(shares, totals))
    first = (me % g) * nr
    mine = (
        lax.broadcasted_iota(jnp.int32, (nr, HD), 0) + first
        == lax.broadcasted_iota(jnp.int32, (nr, HD), 1)
    )
    shares = [jnp.sum(jnp.where(mine, s / total, 0.0), axis=1, keepdims=True) for s in shares]
    with jax.named_scope("owait"):
        for p in range(chips):
            pltpu.make_async_copy(obuf.at[p], obuf.at[p], or_sem.at[p]).wait()
    with jax.named_scope("wwait"):
        ov_copy.wait()
        for i in range(n):
            w_copy(i).wait()

    with jax.named_scope("project"):
        attended = jnp.zeros((nr, HD), F32)
        for p in range(chips):
            attended = attended + shares[p] * obuf[p].astype(F32)
        a = jnp.concatenate([attended[h * rows:(h + 1) * rows] for h in range(hl)], axis=1).astype(BF16)

        def correct(i, part):
            first_block = dest_of(i) * jb
            return jnp.concatenate(
                [
                    part[:, j * HD:(j + 1) * HD] + cbuf[pl.ds(first_block + j, rows, stride=nblocks), :]
                    for j in range(jb)
                ],
                axis=1,
            )

        def p_send(i):
            return pltpu.make_async_remote_copy(
                src_ref=psend.at[i], dst_ref=precv.at[i], send_sem=ps_sem.at[i], recv_sem=pr_sem.at[i],
                device_id={"tensor": partner}, device_id_type=MESH,
            )

        def s_send(i):
            return pltpu.make_async_remote_copy(
                src_ref=sbuf.at[i], dst_ref=rbuf.at[i], send_sem=ss_sem.at[i], recv_sem=sr_sem.at[i],
                device_id={"tensor": 2 * far(i) + core}, device_id_type=MESH,
            )

        acc = None
        cross = chips // 2
        groups = [[(0, k) for k in range(at, min(at + 7, chips - 1))] for at in range(0, chips - 1, 7)]
        groups += [[(1, k) for k in range(at, min(at + 4, cross))] for at in range(0, cross, 4)]
        groups += [[(1, k) for k in range(cross, chips - 2)] + [(0, chips - 1)]]
        groups += [[(1, chips - 2)], [(1, chips - 1)]]
        for turn, group in enumerate(groups):
            if turn == 0:
                none = jnp.zeros((rows, HD), BF16)
                for h in range(0, hl, 2):
                    pair = jnp.concatenate(
                        [
                            jnp.concatenate([a[:, h * HD:(h + 1) * HD], none], axis=1),
                            jnp.concatenate([none, a[:, (h + 1) * HD:(h + 2) * HD]], axis=1),
                        ],
                        axis=0,
                    )
                    blocks = jnp.concatenate(
                        [jnp.concatenate([ovbuf[h, o], ovbuf[h + 1, o]], axis=0) for o in range(omax)], axis=1
                    )
                    both = jnp.dot(pair, blocks, preferred_element_type=F32)
                    for o in range(omax):
                        for e in range(2):
                            at = ((h + e) * omax + o) * rows
                            tbuf[at:at + rows, :] = both[e * rows:(e + 1) * rows, o * HD:(o + 1) * HD]
                pieces = []
                for r in range(rows):
                    term = tbuf[pl.ds(r, terms, stride=rows), :]
                    high = term.astype(BF16)
                    low = (term - high.astype(F32)).astype(BF16)
                    pieces.append(jnp.concatenate([high, low], axis=0))
                placed = jnp.dot(place[...], jnp.concatenate(pieces, axis=1), preferred_element_type=F32)
                for r in range(rows):
                    cbuf[r * nblocks:(r + 1) * nblocks, :] = placed[:, r * HD:(r + 1) * HD]
            parts = [jnp.dot(a, wbuf[2 * k + keep], preferred_element_type=F32) for keep, k in group]
            parts = [correct(2 * k + keep, part) for (keep, k), part in zip(group, parts)]
            for (keep, k), part in zip(group, parts):
                if not keep:
                    psend[k] = part
            for keep, k in group:
                if not keep:
                    p_send(k).start()
            for (keep, k), part in zip(group, parts):
                if keep:
                    with jax.named_scope("pw%d" % k):
                        p_send(k).wait_recv()
                    part = part + precv[k]
                    if k < chips - 1:
                        sbuf[k] = part.astype(BF16)
                        s_send(k).start()
                    else:
                        acc = part

    with jax.named_scope("gather"):
        for i in range(chips):
            target, copy = q_send(i)
            if i < chips // 2 - window:
                pass
            elif i < chips - 1:
                copy.wait_send()
            else:
                pl.when(target != me)(copy.wait_send)
            target, copy = o_send(i)

            @pl.when(target != me)
            def _():
                copy.wait_send()
                t_send(i).wait_send()

            p_send(i).wait_send()
        for i in range(chips - 1):
            s_send(i).wait()
            acc = acc + rbuf[i].astype(F32)
        out_ref[...] = acc.astype(BF16)


def body(n, queries, kv_cache, lengths, out_weight, outlier_values, outlier_columns, outlier_counts):
    rows, width = queries.shape
    hl = width // HD
    nr = hl * rows
    positions = kv_cache.shape[2]
    cols = out_weight.shape[1] // n
    omax = outlier_values.shape[1]
    chips = n // 2
    g = n // KVH
    dma = pltpu.SemaphoreType.DMA
    out = pl.pallas_call(
        functools.partial(kernel, n),
        out_shape=pltpu.VMEM((rows, cols), BF16),
        in_specs=[pl.BlockSpec(memory_space=pl.ANY)] * 7,
        out_specs=pl.BlockSpec(memory_space=pltpu.VMEM),
        scratch_shapes=[
            pltpu.SMEM(lengths.shape, jnp.int32),
            pltpu.SMEM((omax, hl), jnp.int32),
            pltpu.SMEM(outlier_counts.shape, jnp.int32),
            pltpu.VMEM((chips, rows, width), BF16),
            pltpu.VMEM((rows, width), BF16),
            pltpu.VMEM(kv_cache.shape, BF16),
            pltpu.VMEM((2, rows, positions, KVH // 2 * HD), BF16),
            pltpu.VMEM((n, width, cols), BF16),
            pltpu.VMEM(outlier_values.shape, BF16),
            pltpu.VMEM((2, g * nr, rows * positions), F32),
            pltpu.VMEM((2, KVH // 2, HD, rows * positions), BF16),
            pltpu.VMEM((chips, nr, HD), BF16),
            pltpu.VMEM((chips, nr, HD), BF16),
            pltpu.VMEM((chips, 2, HD), F32),
            pltpu.VMEM((chips, 2, HD), F32),
            pltpu.VMEM((hl * omax * rows, HD), F32),
            pltpu.VMEM((n * cols // HD, 2 * hl * omax), BF16),
            pltpu.VMEM((rows * (n * cols // HD), HD), F32),
            pltpu.VMEM((chips, rows, cols), F32),
            pltpu.VMEM((chips, rows, cols), F32),
            pltpu.VMEM((chips, rows, cols), BF16),
            pltpu.VMEM((chips, rows, cols), BF16),
            dma((3,)), dma, dma, dma, dma, dma((chips,)), dma((chips,)), dma((n,)), dma, dma((chips,)), dma((chips,)),
            dma((chips,)), dma((chips,)), dma((chips,)), dma((chips,)), dma((chips,)), dma((chips,)),
        ],
        compiler_params=pltpu.CompilerParams(
            collective_id=0, has_side_effects=True, vmem_limit_bytes=56 * 2**20
        ),
    )(queries, kv_cache, out_weight, outlier_values, lengths, outlier_columns.T, outlier_counts)
    return out


def solution(mesh):
    placed = (
        P("groups", "tensor"),
        P(None, "groups", "tensor", None),
        P("groups"),
        P("tensor", None),
        P("tensor", None, None, None),
        P("tensor", None),
        P("tensor"),
    )
    return jax.shard_map(
        functools.partial(body, mesh.shape["tensor"]),
        mesh=mesh, in_specs=placed, out_specs=P("groups", "tensor"), check_vma=False,
    )
```

```python
import functools
import math

import jax
import jax.numpy as jnp
from jax import lax
from jax.experimental import pallas as pl
from jax.experimental.pallas import tpu as pltpu
from jax.sharding import PartitionSpec as P

KVH = 8
HD = 128
MESH = pl.DeviceIdType.MESH
F32 = jnp.float32
BF16 = jnp.bfloat16


def steps_of(index, n):
    steps, bit = [], 1
    while bit < n:
        steps.append(bit - 2 * bit * ((index // bit) % 2))
        bit *= 2
    return steps


def flip(index, steps, mask):
    for k, step in enumerate(steps):
        if (mask >> k) & 1:
            index = index + step
    return index


def kernel(
    n,
    q_hbm, kv_hbm, w_hbm, ov_hbm, len_hbm, col_hbm, cnt_hbm,
    out_ref,
    len_ref, col_ref, cnt_ref, qbuf, qown, kvown, kvbuf, wbuf, ovbuf, bias, turned, osend, obuf, sstat, rstat, tbuf, place, cbuf,
    psend, precv, sbuf, rbuf,
    small_sem, kv_sem, kvs_sem, kvr_sem, qo_sem, qs_sem, qr_sem, w_sem, ov_sem, os_sem, or_sem, ts_sem, tr_sem,
    ps_sem, pr_sem, ss_sem, sr_sem,
):
    me = lax.axis_index("tensor")
    core = me % 2
    chip = me // 2
    partner = me + 1 - 2 * core
    chips = n // 2
    half = me // chips
    rows, width = q_hbm.shape
    hl = width // HD
    nr = hl * rows
    g = n // KVH
    kh = KVH // 2
    positions = kv_hbm.shape[2]
    cols = w_hbm.shape[1] // n
    omax = ov_hbm.shape[1]
    jb = cols // HD
    hw = kh * HD
    kvcols = rows * positions
    terms = hl * omax
    nblocks = n * jb
    my_slot = me - half * chips
    dev_steps = steps_of(me, n)
    chip_steps = steps_of(chip, chips)

    barrier = pltpu.get_barrier_semaphore()
    for i in range(n - 1, 0, -1):
        pl.semaphore_signal(barrier, inc=1, device_id={"tensor": flip(me, dev_steps, i)}, device_id_type=MESH)

    def far(i):
        return flip(chip, chip_steps, chips - 1 - i)

    other = 1 - (chips - 1 - chip) // (chips - 1)

    def place_of(k):
        if k == chips - 1:
            return chip
        if k == 0:
            return far(0) * (1 - other)
        apart = chips - 1 - chip - k
        return far(k) + other * ((chips * chips - apart * apart) // (chips * chips)) * (far(0) - far(k))

    def dest_of(i):
        return 2 * place_of(i // 2) + (core + 1 + i % 2) % 2

    q_stage = pltpu.make_async_copy(q_hbm, qown, qo_sem)
    q_stage.start()
    kv_own = pltpu.make_async_copy(kv_hbm, kvown, kv_sem)
    kv_own.start()
    small = [
        pltpu.make_async_copy(src, dst, small_sem.at[i])
        for i, (src, dst) in enumerate(((len_hbm, len_ref), (col_hbm, col_ref), (cnt_hbm, cnt_ref)))
    ]
    for copy in small:
        copy.start()

    swap = pltpu.make_async_remote_copy(
        src_ref=kvown.at[:, :, :, pl.ds(pl.multiple_of((1 - core) * hw, hw), hw)], dst_ref=kvbuf, send_sem=kvs_sem, recv_sem=kvr_sem,
        device_id={"tensor": partner}, device_id_type=MESH,
    )

    def q_send(i):
        target = 2 * far(i) + half
        return target, pltpu.make_async_remote_copy(
            src_ref=qown, dst_ref=qbuf.at[my_slot], send_sem=qs_sem.at[i], recv_sem=qr_sem.at[my_slot],
            device_id={"tensor": target}, device_id_type=MESH,
        )

    def w_copy(i):
        return pltpu.make_async_copy(
            w_hbm.at[:, pl.ds(pl.multiple_of(dest_of(i) * cols, cols), cols)], wbuf.at[i], w_sem.at[i]
        )

    ov_copy = pltpu.make_async_copy(ov_hbm, ovbuf, ov_sem)

    @pl.when(me < n)
    def _():
        ov_copy.start()
        for i in range(n):
            w_copy(i).start()

    with jax.named_scope("barrier"):
        q_stage.wait()
        pl.semaphore_wait(barrier, n - 1)

    apart = chips // 2
    window = 3

    def q_start(i):
        target, copy = q_send(i)
        if i < chips - 1:
            copy.start()
        else:
            pl.when(target != me)(copy.start)

    for i in range(window):
        q_start(i)
    kv_own.wait()
    swap.start()

    @pl.when(half == core)
    def _():
        pltpu.make_async_copy(qown, qbuf.at[my_slot], qr_sem.at[my_slot]).start()

    with jax.named_scope("pace"):
        for i in range(window, apart):
            q_send(i - window)[1].wait_send()
            q_start(i)
        for i in range(apart, chips):
            q_start(i)

    with jax.named_scope("masks"):
        for copy in small:
            copy.wait()
        rowreq = lax.broadcasted_iota(jnp.int32, (g * nr, kvcols), 0) % rows
        colidx = lax.broadcasted_iota(jnp.int32, (1, kvcols), 1)
        colreq = colidx // positions
        limit = jnp.zeros((1, kvcols), jnp.int32)
        for r in range(rows):
            limit = jnp.where(colreq == r, len_ref[r], limit)
        for part in range(2):
            dev = me if part == 0 else partner
            live = (colidx % positions + dev * positions) < limit
            tag = jnp.where(live, colreq, -1)
            bias[part] = jnp.where(rowreq == tag, 0.0, -1e30).astype(F32)
        lane = lax.broadcasted_iota(jnp.int32, (nblocks, 2 * terms), 1) % terms
        row = lax.broadcasted_iota(jnp.int32, (nblocks, 2 * terms), 0)
        wanted = jnp.full((nblocks, 2 * terms), -1, jnp.int32)
        for h in range(hl):
            for o in range(omax):
                wanted = jnp.where(lane == h * omax + o, jnp.where(o < cnt_ref[h], col_ref[o, h], -1), wanted)
        place[...] = jnp.where(wanted == row, 1.0, 0.0).astype(BF16)

    with jax.named_scope("turn"):
        for kl in range(kh):
            own_lanes = pl.ds(pl.multiple_of(core * hw + kl * HD, HD), HD)
            turned[0, kl] = kvown[0, :, :, own_lanes].reshape(kvcols, HD).T
    with jax.named_scope("kvwait"):
        swap.wait()
    with jax.named_scope("turn2"):
        for kl in range(kh):
            turned[1, kl] = kvbuf[0, :, :, pl.ds(kl * HD, HD)].reshape(kvcols, HD).T

    eye = lax.broadcasted_iota(jnp.int32, (g * nr, HD), 0) == lax.broadcasted_iota(jnp.int32, (g * nr, HD), 1)

    def to_row(column):
        return jnp.sum(jnp.where(eye, column, 0.0), axis=0, keepdims=True)

    def o_send(j):
        target = core * chips + j
        return target, pltpu.make_async_remote_copy(
            src_ref=osend.at[j], dst_ref=obuf.at[chip], send_sem=os_sem.at[j], recv_sem=or_sem.at[chip],
            device_id={"tensor": target}, device_id_type=MESH,
        )

    def t_send(j):
        return pltpu.make_async_remote_copy(
            src_ref=sstat.at[j], dst_ref=rstat.at[chip], send_sem=ts_sem.at[j], recv_sem=tr_sem.at[chip],
            device_id={"tensor": core * chips + j}, device_id_type=MESH,
        )

    def send_or_keep(j, remote, src, dst, sem):
        target = core * chips + j

        @pl.when(target != me)
        def _():
            remote.start()

        @pl.when(target == me)
        def _():
            pltpu.make_async_copy(src.at[j], dst.at[chip], sem.at[chip]).start()

    kl_here = (chip * 2 // g) % kh
    kl_steps = steps_of(kl_here, kh)
    def attend(kl):
        own_lanes = pl.ds(pl.multiple_of(core * hw + kl * HD, HD), HD)
        lanes = pl.ds(pl.multiple_of(kl * HD, HD), HD)
        pieces = []
        for dl in range(g):
            got = qbuf[kl * g + dl].astype(F32)
            pieces += [got[:, h * HD:(h + 1) * HD] for h in range(hl)]
        q = jnp.concatenate(pieces, axis=0).astype(BF16)
        scores, values = [], []
        for part in range(2):
            held, at = (kvown, own_lanes) if part == 0 else (kvbuf, lanes)
            values.append(held[1, :, :, at].reshape(kvcols, HD))
            s = jnp.dot(q, turned[part, kl], preferred_element_type=F32)
            scores.append(s * (1.0 / math.sqrt(HD)) + bias[part])
        peak = jnp.max(jnp.maximum(scores[0], scores[1]), axis=-1, keepdims=True)
        peak = jnp.maximum(peak, -(2.0**66))
        raised = [jnp.exp(s - peak) for s in scores]
        total = jnp.sum(raised[0] + raised[1], axis=-1, keepdims=True)
        o = jnp.dot(raised[0].astype(BF16), values[0], preferred_element_type=F32)
        o = o + jnp.dot(raised[1].astype(BF16), values[1], preferred_element_type=F32)
        stats = jnp.concatenate([to_row(peak), to_row(total)], axis=0)
        return stats, o.astype(BF16)

    per = 1
    with jax.named_scope("attention"):
        for group in range(0, kh, per):
            kls = [flip(kl_here, kl_steps, kh - 1 - step) for step in range(group, group + per)]
            with jax.named_scope("qw%d" % group):
                for kl in kls:
                    for dl in range(g):
                        slot = kl * g + dl
                        pltpu.make_async_copy(qbuf.at[slot], qbuf.at[slot], qr_sem.at[slot]).wait()
            found = [attend(kl) for kl in kls]
            for kl, (stats, o) in zip(kls, found):
                for dl in range(g):
                    sstat[kl * g + dl] = stats
                    osend[kl * g + dl] = o[dl * nr:(dl + 1) * nr]
            for step, kl in zip(range(group, group + per), kls):
                for dl in range(g):
                    slot = kl * g + dl
                    if step < kh - 1:
                        t_send(slot).start()
                        o_send(slot)[1].start()
                    else:
                        send_or_keep(slot, t_send(slot), sstat, rstat, tr_sem)
                        send_or_keep(slot, o_send(slot)[1], osend, obuf, or_sem)

    with jax.named_scope("twait"):
        for p in range(chips):
            pltpu.make_async_copy(rstat.at[p], rstat.at[p], tr_sem.at[p]).wait()
    peaks = [rstat[p, 0:1, :] for p in range(chips)]
    totals = [rstat[p, 1:2, :] for p in range(chips)]
    peak = functools.reduce(jnp.maximum, peaks)
    shares = [jnp.exp(m - peak) for m in peaks]
    total = sum(s * t for s, t in zip(shares, totals))
    first = (me % g) * nr
    mine = (
        lax.broadcasted_iota(jnp.int32, (nr, HD), 0) + first
        == lax.broadcasted_iota(jnp.int32, (nr, HD), 1)
    )
    shares = [jnp.sum(jnp.where(mine, s / total, 0.0), axis=1, keepdims=True) for s in shares]
    with jax.named_scope("owait"):
        for p in range(chips):
            pltpu.make_async_copy(obuf.at[p], obuf.at[p], or_sem.at[p]).wait()
    with jax.named_scope("wwait"):
        ov_copy.wait()
        for i in range(n):
            w_copy(i).wait()

    with jax.named_scope("project"):
        attended = jnp.zeros((nr, HD), F32)
        for p in range(chips):
            attended = attended + shares[p] * obuf[p].astype(F32)
        a = jnp.concatenate([attended[h * rows:(h + 1) * rows] for h in range(hl)], axis=1).astype(BF16)

        def correct(i, part):
            first_block = dest_of(i) * jb
            return jnp.concatenate(
                [
                    part[:, j * HD:(j + 1) * HD] + cbuf[pl.ds(first_block + j, rows, stride=nblocks), :]
                    for j in range(jb)
                ],
                axis=1,
            )

        def p_send(i):
            return pltpu.make_async_remote_copy(
                src_ref=psend.at[i], dst_ref=precv.at[i], send_sem=ps_sem.at[i], recv_sem=pr_sem.at[i],
                device_id={"tensor": partner}, device_id_type=MESH,
            )

        def s_send(i):
            return pltpu.make_async_remote_copy(
                src_ref=sbuf.at[i], dst_ref=rbuf.at[chip], send_sem=ss_sem.at[i], recv_sem=sr_sem.at[chip],
                device_id={"tensor": 2 * place_of(i) + core}, device_id_type=MESH,
            )

        acc = None
        cross = chips // 2
        groups = [
            [(0, k) for k in range(cross)],
            [(1, 0)] + [(0, k) for k in range(cross, chips)],
            [(1, k) for k in range(1, cross)],
            [(1, k) for k in range(cross, chips - 1)],
            [(1, chips - 1)],
        ]
        for turn, group in enumerate(groups):
            if turn == 0:
                none = jnp.zeros((rows, HD), BF16)
                for h in range(0, hl, 2):
                    pair = jnp.concatenate(
                        [
                            jnp.concatenate([a[:, h * HD:(h + 1) * HD], none], axis=1),
                            jnp.concatenate([none, a[:, (h + 1) * HD:(h + 2) * HD]], axis=1),
                        ],
                        axis=0,
                    )
                    blocks = jnp.concatenate(
                        [jnp.concatenate([ovbuf[h, o], ovbuf[h + 1, o]], axis=0) for o in range(omax)], axis=1
                    )
                    both = jnp.dot(pair, blocks, preferred_element_type=F32)
                    for o in range(omax):
                        for e in range(2):
                            at = ((h + e) * omax + o) * rows
                            tbuf[at:at + rows, :] = both[e * rows:(e + 1) * rows, o * HD:(o + 1) * HD]
                pieces = []
                for r in range(rows):
                    term = tbuf[pl.ds(r, terms, stride=rows), :]
                    high = term.astype(BF16)
                    low = (term - high.astype(F32)).astype(BF16)
                    pieces.append(jnp.concatenate([high, low], axis=0))
                placed = jnp.dot(place[...], jnp.concatenate(pieces, axis=1), preferred_element_type=F32)
                for r in range(rows):
                    cbuf[r * nblocks:(r + 1) * nblocks, :] = placed[:, r * HD:(r + 1) * HD]
            parts = [jnp.dot(a, wbuf[2 * k + keep], preferred_element_type=F32) for keep, k in group]
            parts = [correct(2 * k + keep, part) for (keep, k), part in zip(group, parts)]
            for (keep, k), part in zip(group, parts):
                if not keep:
                    psend[k] = part
            for keep, k in group:
                if not keep:
                    p_send(k).start()
            for (keep, k), part in zip(group, parts):
                if keep:
                    with jax.named_scope("pw%d" % k):
                        p_send(k).wait_recv()
                    part = part + precv[k]
                    if k < chips - 1:
                        sbuf[k] = part.astype(BF16)
                        s_send(k).start()
                    else:
                        acc = part

    with jax.named_scope("gather"):
        for i in range(chips):
            target, copy = q_send(i)
            if i < chips // 2 - window:
                pass
            elif i < chips - 1:
                copy.wait_send()
            else:
                pl.when(target != me)(copy.wait_send)
            target, copy = o_send(i)

            @pl.when(target != me)
            def _():
                copy.wait_send()
                t_send(i).wait_send()

            p_send(i).wait_send()
        for i in range(chips - 1):
            s_send(i).wait_send()
        for mask in range(1, chips):
            p = flip(chip, chip_steps, mask)
            pltpu.make_async_copy(rbuf.at[p], rbuf.at[p], sr_sem.at[p]).wait()
            acc = acc + rbuf[p].astype(F32)
        out_ref[...] = acc.astype(BF16)


def body(n, queries, kv_cache, lengths, out_weight, outlier_values, outlier_columns, outlier_counts):
    rows, width = queries.shape
    hl = width // HD
    nr = hl * rows
    positions = kv_cache.shape[2]
    cols = out_weight.shape[1] // n
    omax = outlier_values.shape[1]
    chips = n // 2
    g = n // KVH
    dma = pltpu.SemaphoreType.DMA
    out = pl.pallas_call(
        functools.partial(kernel, n),
        out_shape=pltpu.VMEM((rows, cols), BF16),
        in_specs=[pl.BlockSpec(memory_space=pl.ANY)] * 7,
        out_specs=pl.BlockSpec(memory_space=pltpu.VMEM),
        scratch_shapes=[
            pltpu.SMEM(lengths.shape, jnp.int32),
            pltpu.SMEM((omax, hl), jnp.int32),
            pltpu.SMEM(outlier_counts.shape, jnp.int32),
            pltpu.VMEM((chips, rows, width), BF16),
            pltpu.VMEM((rows, width), BF16),
            pltpu.VMEM(kv_cache.shape, BF16),
            pltpu.VMEM((2, rows, positions, KVH // 2 * HD), BF16),
            pltpu.VMEM((n, width, cols), BF16),
            pltpu.VMEM(outlier_values.shape, BF16),
            pltpu.VMEM((2, g * nr, rows * positions), F32),
            pltpu.VMEM((2, KVH // 2, HD, rows * positions), BF16),
            pltpu.VMEM((chips, nr, HD), BF16),
            pltpu.VMEM((chips, nr, HD), BF16),
            pltpu.VMEM((chips, 2, HD), F32),
            pltpu.VMEM((chips, 2, HD), F32),
            pltpu.VMEM((hl * omax * rows, HD), F32),
            pltpu.VMEM((n * cols // HD, 2 * hl * omax), BF16),
            pltpu.VMEM((rows * (n * cols // HD), HD), F32),
            pltpu.VMEM((chips, rows, cols), F32),
            pltpu.VMEM((chips, rows, cols), F32),
            pltpu.VMEM((chips, rows, cols), BF16),
            pltpu.VMEM((chips, rows, cols), BF16),
            dma((3,)), dma, dma, dma, dma, dma((chips,)), dma((chips,)), dma((n,)), dma, dma((chips,)), dma((chips,)),
            dma((chips,)), dma((chips,)), dma((chips,)), dma((chips,)), dma((chips,)), dma((chips,)),
        ],
        compiler_params=pltpu.CompilerParams(
            collective_id=0, has_side_effects=True, vmem_limit_bytes=56 * 2**20
        ),
    )(queries, kv_cache, out_weight, outlier_values, lengths, outlier_columns.T, outlier_counts)
    return out


def solution(mesh):
    placed = (
        P("groups", "tensor"),
        P(None, "groups", "tensor", None),
        P("groups"),
        P("tensor", None),
        P("tensor", None, None, None),
        P("tensor", None),
        P("tensor"),
    )
    return jax.shard_map(
        functools.partial(body, mesh.shape["tensor"]),
        mesh=mesh, in_specs=placed, out_specs=P("groups", "tensor"), check_vma=False,
    )
```

```python
import functools
import math

import jax
import jax.numpy as jnp
from jax import lax
from jax.experimental import pallas as pl
from jax.experimental.pallas import tpu as pltpu
from jax.sharding import PartitionSpec as P

KVH = 8
HD = 128
MESH = pl.DeviceIdType.MESH
F32 = jnp.float32
BF16 = jnp.bfloat16


def steps_of(index, n):
    steps, bit = [], 1
    while bit < n:
        steps.append(bit - 2 * bit * ((index // bit) % 2))
        bit *= 2
    return steps


def flip(index, steps, mask):
    for k, step in enumerate(steps):
        if (mask >> k) & 1:
            index = index + step
    return index


def kernel(
    n,
    q_hbm, kv_hbm, w_hbm, ov_hbm, len_hbm, col_hbm, cnt_hbm,
    out_ref,
    len_ref, col_ref, cnt_ref, qbuf, qown, kvown, kvbuf, wbuf, ovbuf, bias, turned, osend, obuf, sstat, rstat, tbuf, place, cbuf,
    psend, precv, sbuf, rbuf,
    small_sem, kv_sem, kvs_sem, kvr_sem, qo_sem, qs_sem, qr_sem, w_sem, ov_sem, os_sem, or_sem, ts_sem, tr_sem,
    ps_sem, pr_sem, ss_sem, sr_sem,
):
    me = lax.axis_index("tensor")
    core = me % 2
    chip = me // 2
    partner = me + 1 - 2 * core
    chips = n // 2
    half = me // chips
    rows, width = q_hbm.shape
    hl = width // HD
    nr = hl * rows
    g = n // KVH
    kh = KVH // 2
    positions = kv_hbm.shape[2]
    cols = w_hbm.shape[1] // n
    omax = ov_hbm.shape[1]
    jb = cols // HD
    hw = kh * HD
    kvcols = rows * positions
    terms = hl * omax
    nblocks = n * jb
    my_slot = me - half * chips
    dev_steps = steps_of(me, n)
    chip_steps = steps_of(chip, chips)

    barrier = pltpu.get_barrier_semaphore()
    for i in range(n - 1, 0, -1):
        pl.semaphore_signal(barrier, inc=1, device_id={"tensor": flip(me, dev_steps, i)}, device_id_type=MESH)

    def far(i):
        return flip(chip, chip_steps, chips - 1 - i)

    other = 1 - (chips - 1 - chip) // (chips - 1)

    def place_of(k):
        if k == chips - 1:
            return chip
        if k == 0:
            return far(0) * (1 - other)
        apart = chips - 1 - chip - k
        return far(k) + other * ((chips * chips - apart * apart) // (chips * chips)) * (far(0) - far(k))

    def dest_of(i):
        return 2 * place_of(i // 2) + (core + 1 + i % 2) % 2

    q_stage = pltpu.make_async_copy(q_hbm, qown, qo_sem)
    q_stage.start()
    kv_own = pltpu.make_async_copy(kv_hbm, kvown, kv_sem)
    kv_own.start()
    small = [
        pltpu.make_async_copy(src, dst, small_sem.at[i])
        for i, (src, dst) in enumerate(((len_hbm, len_ref), (col_hbm, col_ref), (cnt_hbm, cnt_ref)))
    ]
    for copy in small:
        copy.start()

    swap = pltpu.make_async_remote_copy(
        src_ref=kvown.at[:, :, :, pl.ds(pl.multiple_of((1 - core) * hw, hw), hw)], dst_ref=kvbuf, send_sem=kvs_sem, recv_sem=kvr_sem,
        device_id={"tensor": partner}, device_id_type=MESH,
    )

    def q_send(i):
        target = 2 * far(i) + half
        return target, pltpu.make_async_remote_copy(
            src_ref=qown, dst_ref=qbuf.at[my_slot], send_sem=qs_sem.at[i], recv_sem=qr_sem.at[my_slot],
            device_id={"tensor": target}, device_id_type=MESH,
        )

    def w_copy(i):
        return pltpu.make_async_copy(
            w_hbm.at[:, pl.ds(pl.multiple_of(dest_of(i) * cols, cols), cols)], wbuf.at[i], w_sem.at[i]
        )

    ov_copy = pltpu.make_async_copy(ov_hbm, ovbuf, ov_sem)

    @pl.when(me < n)
    def _():
        ov_copy.start()
        for i in range(n):
            w_copy(i).start()

    with jax.named_scope("barrier"):
        q_stage.wait()
        pl.semaphore_wait(barrier, n - 1)

    apart = chips // 2
    window = 3

    def q_start(i):
        target, copy = q_send(i)
        if i < chips - 1:
            copy.start()
        else:
            pl.when(target != me)(copy.start)

    for i in range(window):
        q_start(i)
    kv_own.wait()
    swap.start()

    @pl.when(half == core)
    def _():
        pltpu.make_async_copy(qown, qbuf.at[my_slot], qr_sem.at[my_slot]).start()

    with jax.named_scope("pace"):
        for i in range(window, apart):
            q_send(i - window)[1].wait_send()
            q_start(i)
        for i in range(apart, chips):
            q_start(i)

    with jax.named_scope("masks"):
        for copy in small:
            copy.wait()
        rowreq = lax.broadcasted_iota(jnp.int32, (g * nr, kvcols), 0) % rows
        colidx = lax.broadcasted_iota(jnp.int32, (1, kvcols), 1)
        colreq = colidx // positions
        limit = jnp.zeros((1, kvcols), jnp.int32)
        for r in range(rows):
            limit = jnp.where(colreq == r, len_ref[r], limit)
        for part in range(2):
            dev = me if part == 0 else partner
            live = (colidx % positions + dev * positions) < limit
            tag = jnp.where(live, colreq, -1)
            bias[part] = jnp.where(rowreq == tag, 0.0, -1e30).astype(F32)
        lane = lax.broadcasted_iota(jnp.int32, (nblocks, 2 * terms), 1) % terms
        row = lax.broadcasted_iota(jnp.int32, (nblocks, 2 * terms), 0)
        wanted = jnp.full((nblocks, 2 * terms), -1, jnp.int32)
        for h in range(hl):
            for o in range(omax):
                wanted = jnp.where(lane == h * omax + o, jnp.where(o < cnt_ref[h], col_ref[o, h], -1), wanted)
        place[...] = jnp.where(wanted == row, 1.0, 0.0).astype(BF16)

    with jax.named_scope("turn"):
        for kl in range(kh):
            own_lanes = pl.ds(pl.multiple_of(core * hw + kl * HD, HD), HD)
            turned[0, kl] = kvown[0, :, :, own_lanes].reshape(kvcols, HD).T
    with jax.named_scope("kvwait"):
        swap.wait()
    with jax.named_scope("turn2"):
        for kl in range(kh):
            turned[1, kl] = kvbuf[0, :, :, pl.ds(kl * HD, HD)].reshape(kvcols, HD).T

    eye = lax.broadcasted_iota(jnp.int32, (g * nr, HD), 0) == lax.broadcasted_iota(jnp.int32, (g * nr, HD), 1)

    def to_row(column):
        return jnp.sum(jnp.where(eye, column, 0.0), axis=0, keepdims=True)

    def o_send(j):
        target = core * chips + j
        return target, pltpu.make_async_remote_copy(
            src_ref=osend.at[j], dst_ref=obuf.at[chip], send_sem=os_sem.at[j], recv_sem=or_sem.at[chip],
            device_id={"tensor": target}, device_id_type=MESH,
        )

    def t_send(j):
        return pltpu.make_async_remote_copy(
            src_ref=sstat.at[j], dst_ref=rstat.at[chip], send_sem=ts_sem.at[j], recv_sem=tr_sem.at[chip],
            device_id={"tensor": core * chips + j}, device_id_type=MESH,
        )

    def send_or_keep(j, remote, src, dst, sem):
        target = core * chips + j

        @pl.when(target != me)
        def _():
            remote.start()

        @pl.when(target == me)
        def _():
            pltpu.make_async_copy(src.at[j], dst.at[chip], sem.at[chip]).start()

    kl_here = (chip * 2 // g) % kh
    kl_steps = steps_of(kl_here, kh)
    def attend(kl):
        own_lanes = pl.ds(pl.multiple_of(core * hw + kl * HD, HD), HD)
        lanes = pl.ds(pl.multiple_of(kl * HD, HD), HD)
        pieces = []
        for dl in range(g):
            got = qbuf[kl * g + dl].astype(F32)
            pieces += [got[:, h * HD:(h + 1) * HD] for h in range(hl)]
        q = jnp.concatenate(pieces, axis=0).astype(BF16)
        scores, values = [], []
        for part in range(2):
            held, at = (kvown, own_lanes) if part == 0 else (kvbuf, lanes)
            values.append(held[1, :, :, at].reshape(kvcols, HD))
            s = jnp.dot(q, turned[part, kl], preferred_element_type=F32)
            scores.append(s * (1.0 / math.sqrt(HD)) + bias[part])
        peak = jnp.max(jnp.maximum(scores[0], scores[1]), axis=-1, keepdims=True)
        peak = jnp.maximum(peak, -(2.0**66))
        raised = [jnp.exp(s - peak) for s in scores]
        total = jnp.sum(raised[0] + raised[1], axis=-1, keepdims=True)
        o = jnp.dot(raised[0].astype(BF16), values[0], preferred_element_type=F32)
        o = o + jnp.dot(raised[1].astype(BF16), values[1], preferred_element_type=F32)
        stats = jnp.concatenate([to_row(peak), to_row(total)], axis=0)
        return stats, o.astype(BF16)

    per = 1
    with jax.named_scope("attention"):
        for group in range(0, kh, per):
            kls = [flip(kl_here, kl_steps, kh - 1 - step) for step in range(group, group + per)]
            with jax.named_scope("qw%d" % group):
                for kl in kls:
                    for dl in range(g):
                        slot = kl * g + dl
                        pltpu.make_async_copy(qbuf.at[slot], qbuf.at[slot], qr_sem.at[slot]).wait()
            found = [attend(kl) for kl in kls]
            for kl, (stats, o) in zip(kls, found):
                for dl in range(g):
                    sstat[kl * g + dl] = stats
                    osend[kl * g + dl] = o[dl * nr:(dl + 1) * nr]
            for step, kl in zip(range(group, group + per), kls):
                for dl in range(g):
                    slot = kl * g + dl
                    if step < kh - 1:
                        t_send(slot).start()
                        o_send(slot)[1].start()
                    else:
                        send_or_keep(slot, t_send(slot), sstat, rstat, tr_sem)
                        send_or_keep(slot, o_send(slot)[1], osend, obuf, or_sem)

    with jax.named_scope("twait"):
        for p in range(chips):
            pltpu.make_async_copy(rstat.at[p], rstat.at[p], tr_sem.at[p]).wait()
    peaks = [rstat[p, 0:1, :] for p in range(chips)]
    totals = [rstat[p, 1:2, :] for p in range(chips)]
    peak = functools.reduce(jnp.maximum, peaks)
    shares = [jnp.exp(m - peak) for m in peaks]
    total = sum(s * t for s, t in zip(shares, totals))
    first = (me % g) * nr
    mine = (
        lax.broadcasted_iota(jnp.int32, (nr, HD), 0) + first
        == lax.broadcasted_iota(jnp.int32, (nr, HD), 1)
    )
    shares = [jnp.sum(jnp.where(mine, s / total, 0.0), axis=1, keepdims=True) for s in shares]
    with jax.named_scope("owait"):
        for p in range(chips):
            pltpu.make_async_copy(obuf.at[p], obuf.at[p], or_sem.at[p]).wait()
    with jax.named_scope("wwait"):
        ov_copy.wait()
        for i in range(n):
            w_copy(i).wait()

    with jax.named_scope("project"):
        attended = jnp.zeros((nr, HD), F32)
        for p in range(chips):
            attended = attended + shares[p] * obuf[p].astype(F32)
        a = jnp.concatenate([attended[h * rows:(h + 1) * rows] for h in range(hl)], axis=1).astype(BF16)

        def correct(i, part):
            first_block = dest_of(i) * jb
            return jnp.concatenate(
                [
                    part[:, j * HD:(j + 1) * HD] + cbuf[pl.ds(first_block + j, rows, stride=nblocks), :]
                    for j in range(jb)
                ],
                axis=1,
            )

        def p_send(i):
            return pltpu.make_async_remote_copy(
                src_ref=psend.at[i], dst_ref=precv.at[i], send_sem=ps_sem.at[i], recv_sem=pr_sem.at[i],
                device_id={"tensor": partner}, device_id_type=MESH,
            )

        def s_send(i):
            return pltpu.make_async_remote_copy(
                src_ref=sbuf.at[i], dst_ref=rbuf.at[chip], send_sem=ss_sem.at[i], recv_sem=sr_sem.at[chip],
                device_id={"tensor": 2 * place_of(i) + core}, device_id_type=MESH,
            )

        acc = None
        cross = chips // 2
        groups = [
            [(0, k) for k in range(cross)],
            [(1, 0)] + [(0, k) for k in range(cross, chips - 1)],
            [(1, k) for k in range(1, cross)] + [(0, chips - 1)],
            [(1, k) for k in range(cross, chips - 1)],
            [(1, chips - 1)],
        ]
        for turn, group in enumerate(groups):
            if turn == 0:
                none = jnp.zeros((rows, HD), BF16)
                for h in range(0, hl, 2):
                    pair = jnp.concatenate(
                        [
                            jnp.concatenate([a[:, h * HD:(h + 1) * HD], none], axis=1),
                            jnp.concatenate([none, a[:, (h + 1) * HD:(h + 2) * HD]], axis=1),
                        ],
                        axis=0,
                    )
                    blocks = jnp.concatenate(
                        [jnp.concatenate([ovbuf[h, o], ovbuf[h + 1, o]], axis=0) for o in range(omax)], axis=1
                    )
                    both = jnp.dot(pair, blocks, preferred_element_type=F32)
                    for o in range(omax):
                        for e in range(2):
                            at = ((h + e) * omax + o) * rows
                            tbuf[at:at + rows, :] = both[e * rows:(e + 1) * rows, o * HD:(o + 1) * HD]
                pieces = []
                for r in range(rows):
                    term = tbuf[pl.ds(r, terms, stride=rows), :]
                    high = term.astype(BF16)
                    low = (term - high.astype(F32)).astype(BF16)
                    pieces.append(jnp.concatenate([high, low], axis=0))
                placed = jnp.dot(place[...], jnp.concatenate(pieces, axis=1), preferred_element_type=F32)
                for r in range(rows):
                    cbuf[r * nblocks:(r + 1) * nblocks, :] = placed[:, r * HD:(r + 1) * HD]
            parts = [jnp.dot(a, wbuf[2 * k + keep], preferred_element_type=F32) for keep, k in group]
            parts = [correct(2 * k + keep, part) for (keep, k), part in zip(group, parts)]
            for (keep, k), part in zip(group, parts):
                if not keep:
                    psend[k] = part
            for keep, k in group:
                if not keep:
                    p_send(k).start()
            for (keep, k), part in zip(group, parts):
                if keep:
                    with jax.named_scope("pw%d" % k):
                        p_send(k).wait_recv()
                    part = part + precv[k]
                    if k < chips - 1:
                        sbuf[k] = part.astype(BF16)
                        s_send(k).start()
                    else:
                        acc = part

    with jax.named_scope("gather"):
        for i in range(chips):
            target, copy = q_send(i)
            if i < chips // 2 - window:
                pass
            elif i < chips - 1:
                copy.wait_send()
            else:
                pl.when(target != me)(copy.wait_send)
            target, copy = o_send(i)

            @pl.when(target != me)
            def _():
                copy.wait_send()
                t_send(i).wait_send()

            p_send(i).wait_send()
        for i in range(chips - 1):
            s_send(i).wait_send()
        for mask in range(1, chips):
            p = flip(chip, chip_steps, mask)
            pltpu.make_async_copy(rbuf.at[p], rbuf.at[p], sr_sem.at[p]).wait()
            acc = acc + rbuf[p].astype(F32)
        out_ref[...] = acc.astype(BF16)


def body(n, queries, kv_cache, lengths, out_weight, outlier_values, outlier_columns, outlier_counts):
    rows, width = queries.shape
    hl = width // HD
    nr = hl * rows
    positions = kv_cache.shape[2]
    cols = out_weight.shape[1] // n
    omax = outlier_values.shape[1]
    chips = n // 2
    g = n // KVH
    dma = pltpu.SemaphoreType.DMA
    out = pl.pallas_call(
        functools.partial(kernel, n),
        out_shape=pltpu.VMEM((rows, cols), BF16),
        in_specs=[pl.BlockSpec(memory_space=pl.ANY)] * 7,
        out_specs=pl.BlockSpec(memory_space=pltpu.VMEM),
        scratch_shapes=[
            pltpu.SMEM(lengths.shape, jnp.int32),
            pltpu.SMEM((omax, hl), jnp.int32),
            pltpu.SMEM(outlier_counts.shape, jnp.int32),
            pltpu.VMEM((chips, rows, width), BF16),
            pltpu.VMEM((rows, width), BF16),
            pltpu.VMEM(kv_cache.shape, BF16),
            pltpu.VMEM((2, rows, positions, KVH // 2 * HD), BF16),
            pltpu.VMEM((n, width, cols), BF16),
            pltpu.VMEM(outlier_values.shape, BF16),
            pltpu.VMEM((2, g * nr, rows * positions), F32),
            pltpu.VMEM((2, KVH // 2, HD, rows * positions), BF16),
            pltpu.VMEM((chips, nr, HD), BF16),
            pltpu.VMEM((chips, nr, HD), BF16),
            pltpu.VMEM((chips, 2, HD), F32),
            pltpu.VMEM((chips, 2, HD), F32),
            pltpu.VMEM((hl * omax * rows, HD), F32),
            pltpu.VMEM((n * cols // HD, 2 * hl * omax), BF16),
            pltpu.VMEM((rows * (n * cols // HD), HD), F32),
            pltpu.VMEM((chips, rows, cols), F32),
            pltpu.VMEM((chips, rows, cols), F32),
            pltpu.VMEM((chips, rows, cols), BF16),
            pltpu.VMEM((chips, rows, cols), BF16),
            dma((3,)), dma, dma, dma, dma, dma((chips,)), dma((chips,)), dma((n,)), dma, dma((chips,)), dma((chips,)),
            dma((chips,)), dma((chips,)), dma((chips,)), dma((chips,)), dma((chips,)), dma((chips,)),
        ],
        compiler_params=pltpu.CompilerParams(
            collective_id=0, has_side_effects=True, vmem_limit_bytes=56 * 2**20
        ),
    )(queries, kv_cache, out_weight, outlier_values, lengths, outlier_columns.T, outlier_counts)
    return out


def solution(mesh):
    placed = (
        P("groups", "tensor"),
        P(None, "groups", "tensor", None),
        P("groups"),
        P("tensor", None),
        P("tensor", None, None, None),
        P("tensor", None),
        P("tensor"),
    )
    return jax.shard_map(
        functools.partial(body, mesh.shape["tensor"]),
        mesh=mesh, in_specs=placed, out_specs=P("groups", "tensor"), check_vma=False,
    )
```

```python
import functools
import math

import jax
import jax.numpy as jnp
from jax import lax
from jax.experimental import pallas as pl
from jax.experimental.pallas import tpu as pltpu
from jax.sharding import PartitionSpec as P

KVH = 8
HD = 128
MESH = pl.DeviceIdType.MESH
F32 = jnp.float32
BF16 = jnp.bfloat16


def steps_of(index, n):
    steps, bit = [], 1
    while bit < n:
        steps.append(bit - 2 * bit * ((index // bit) % 2))
        bit *= 2
    return steps


def flip(index, steps, mask):
    for k, step in enumerate(steps):
        if (mask >> k) & 1:
            index = index + step
    return index


def kernel(
    n,
    q_hbm, kv_hbm, w_hbm, ov_hbm, len_hbm, col_hbm, cnt_hbm,
    out_ref,
    len_ref, col_ref, cnt_ref, qbuf, qown, kvown, kvbuf, wbuf, ovbuf, bias, turned, osend, obuf, sstat, rstat, tbuf, place, cbuf,
    psend, precv, sbuf, rbuf,
    small_sem, kv_sem, kvs_sem, kvr_sem, qo_sem, qs_sem, qr_sem, w_sem, ov_sem, os_sem, or_sem, ts_sem, tr_sem,
    ps_sem, pr_sem, ss_sem, sr_sem,
):
    me = lax.axis_index("tensor")
    core = me % 2
    chip = me // 2
    partner = me + 1 - 2 * core
    chips = n // 2
    half = me // chips
    rows, width = q_hbm.shape
    hl = width // HD
    nr = hl * rows
    g = n // KVH
    kh = KVH // 2
    positions = kv_hbm.shape[2]
    cols = w_hbm.shape[1] // n
    omax = ov_hbm.shape[1]
    jb = cols // HD
    hw = kh * HD
    kvcols = rows * positions
    terms = hl * omax
    nblocks = n * jb
    my_slot = me - half * chips
    dev_steps = steps_of(me, n)
    chip_steps = steps_of(chip, chips)

    barrier = pltpu.get_barrier_semaphore()
    slot_steps = steps_of(my_slot, chips)

    def ready(target):
        pl.semaphore_signal(barrier, inc=1, device_id={"tensor": target}, device_id_type=MESH)

    for i in range(chips - 1, 0, -1):
        ready(core * chips + flip(my_slot, slot_steps, i))

    @pl.when(half != core)
    def _():
        ready(core * chips + my_slot)
        ready(partner)

    def far(i):
        return flip(chip, chip_steps, chips - 1 - i)

    other = 1 - (chips - 1 - chip) // (chips - 1)

    def place_of(k):
        if k == chips - 1:
            return chip
        if k == 0:
            return far(0) * (1 - other)
        apart = chips - 1 - chip - k
        return far(k) + other * ((chips * chips - apart * apart) // (chips * chips)) * (far(0) - far(k))

    def dest_of(i):
        return 2 * place_of(i // 2) + (core + 1 + i % 2) % 2

    q_stage = pltpu.make_async_copy(q_hbm, qown, qo_sem)
    q_stage.start()
    kv_own = pltpu.make_async_copy(kv_hbm, kvown, kv_sem)
    kv_own.start()
    small = [
        pltpu.make_async_copy(src, dst, small_sem.at[i])
        for i, (src, dst) in enumerate(((len_hbm, len_ref), (col_hbm, col_ref), (cnt_hbm, cnt_ref)))
    ]
    for copy in small:
        copy.start()

    swap = pltpu.make_async_remote_copy(
        src_ref=kvown.at[:, :, :, pl.ds(pl.multiple_of((1 - core) * hw, hw), hw)], dst_ref=kvbuf, send_sem=kvs_sem, recv_sem=kvr_sem,
        device_id={"tensor": partner}, device_id_type=MESH,
    )

    def q_send(i):
        target = 2 * far(i) + half
        return target, pltpu.make_async_remote_copy(
            src_ref=qown, dst_ref=qbuf.at[my_slot], send_sem=qs_sem.at[i], recv_sem=qr_sem.at[my_slot],
            device_id={"tensor": target}, device_id_type=MESH,
        )

    def w_copy(i):
        return pltpu.make_async_copy(
            w_hbm.at[:, pl.ds(pl.multiple_of(dest_of(i) * cols, cols), cols)], wbuf.at[i], w_sem.at[i]
        )

    ov_copy = pltpu.make_async_copy(ov_hbm, ovbuf, ov_sem)

    @pl.when(me < n)
    def _():
        ov_copy.start()
        for i in range(n):
            w_copy(i).start()

    with jax.named_scope("barrier"):
        q_stage.wait()
        pl.semaphore_wait(barrier, chips)

    apart = chips // 2
    window = 3

    def q_start(i):
        target, copy = q_send(i)
        if i < chips - 1:
            copy.start()
        else:
            pl.when(target != me)(copy.start)

    for i in range(window):
        q_start(i)
    kv_own.wait()
    swap.start()

    @pl.when(half == core)
    def _():
        pltpu.make_async_copy(qown, qbuf.at[my_slot], qr_sem.at[my_slot]).start()

    with jax.named_scope("pace"):
        for i in range(window, apart):
            q_send(i - window)[1].wait_send()
            q_start(i)
        for i in range(apart, chips):
            q_start(i)

    with jax.named_scope("masks"):
        for copy in small:
            copy.wait()
        rowreq = lax.broadcasted_iota(jnp.int32, (g * nr, kvcols), 0) % rows
        colidx = lax.broadcasted_iota(jnp.int32, (1, kvcols), 1)
        colreq = colidx // positions
        limit = jnp.zeros((1, kvcols), jnp.int32)
        for r in range(rows):
            limit = jnp.where(colreq == r, len_ref[r], limit)
        for part in range(2):
            dev = me if part == 0 else partner
            live = (colidx % positions + dev * positions) < limit
            tag = jnp.where(live, colreq, -1)
            bias[part] = jnp.where(rowreq == tag, 0.0, -1e30).astype(F32)
        lane = lax.broadcasted_iota(jnp.int32, (nblocks, 2 * terms), 1) % terms
        row = lax.broadcasted_iota(jnp.int32, (nblocks, 2 * terms), 0)
        wanted = jnp.full((nblocks, 2 * terms), -1, jnp.int32)
        for h in range(hl):
            for o in range(omax):
                wanted = jnp.where(lane == h * omax + o, jnp.where(o < cnt_ref[h], col_ref[o, h], -1), wanted)
        place[...] = jnp.where(wanted == row, 1.0, 0.0).astype(BF16)

    with jax.named_scope("turn"):
        for kl in range(kh):
            own_lanes = pl.ds(pl.multiple_of(core * hw + kl * HD, HD), HD)
            turned[0, kl] = kvown[0, :, :, own_lanes].reshape(kvcols, HD).T
    with jax.named_scope("kvwait"):
        swap.wait()
    with jax.named_scope("turn2"):
        for kl in range(kh):
            turned[1, kl] = kvbuf[0, :, :, pl.ds(kl * HD, HD)].reshape(kvcols, HD).T

    eye = lax.broadcasted_iota(jnp.int32, (g * nr, HD), 0) == lax.broadcasted_iota(jnp.int32, (g * nr, HD), 1)

    def to_row(column):
        return jnp.sum(jnp.where(eye, column, 0.0), axis=0, keepdims=True)

    def o_send(j):
        target = core * chips + j
        return target, pltpu.make_async_remote_copy(
            src_ref=osend.at[j], dst_ref=obuf.at[chip], send_sem=os_sem.at[j], recv_sem=or_sem.at[chip],
            device_id={"tensor": target}, device_id_type=MESH,
        )

    def t_send(j):
        return pltpu.make_async_remote_copy(
            src_ref=sstat.at[j], dst_ref=rstat.at[chip], send_sem=ts_sem.at[j], recv_sem=tr_sem.at[chip],
            device_id={"tensor": core * chips + j}, device_id_type=MESH,
        )

    def send_or_keep(j, remote, src, dst, sem):
        target = core * chips + j

        @pl.when(target != me)
        def _():
            remote.start()

        @pl.when(target == me)
        def _():
            pltpu.make_async_copy(src.at[j], dst.at[chip], sem.at[chip]).start()

    kl_here = (chip * 2 // g) % kh
    kl_steps = steps_of(kl_here, kh)
    def attend(kl):
        own_lanes = pl.ds(pl.multiple_of(core * hw + kl * HD, HD), HD)
        lanes = pl.ds(pl.multiple_of(kl * HD, HD), HD)
        pieces = []
        for dl in range(g):
            got = qbuf[kl * g + dl].astype(F32)
            pieces += [got[:, h * HD:(h + 1) * HD] for h in range(hl)]
        q = jnp.concatenate(pieces, axis=0).astype(BF16)
        scores, values = [], []
        for part in range(2):
            held, at = (kvown, own_lanes) if part == 0 else (kvbuf, lanes)
            values.append(held[1, :, :, at].reshape(kvcols, HD))
            s = jnp.dot(q, turned[part, kl], preferred_element_type=F32)
            scores.append(s * (1.0 / math.sqrt(HD)) + bias[part])
        peak = jnp.max(jnp.maximum(scores[0], scores[1]), axis=-1, keepdims=True)
        peak = jnp.maximum(peak, -(2.0**66))
        raised = [jnp.exp(s - peak) for s in scores]
        total = jnp.sum(raised[0] + raised[1], axis=-1, keepdims=True)
        o = jnp.dot(raised[0].astype(BF16), values[0], preferred_element_type=F32)
        o = o + jnp.dot(raised[1].astype(BF16), values[1], preferred_element_type=F32)
        stats = jnp.concatenate([to_row(peak), to_row(total)], axis=0)
        return stats, o.astype(BF16)

    per = 1
    with jax.named_scope("attention"):
        for group in range(0, kh, per):
            kls = [flip(kl_here, kl_steps, kh - 1 - step) for step in range(group, group + per)]
            with jax.named_scope("qw%d" % group):
                for kl in kls:
                    for dl in range(g):
                        slot = kl * g + dl
                        pltpu.make_async_copy(qbuf.at[slot], qbuf.at[slot], qr_sem.at[slot]).wait()
            found = [attend(kl) for kl in kls]
            for kl, (stats, o) in zip(kls, found):
                for dl in range(g):
                    sstat[kl * g + dl] = stats
                    osend[kl * g + dl] = o[dl * nr:(dl + 1) * nr]
            for step, kl in zip(range(group, group + per), kls):
                for dl in range(g):
                    slot = kl * g + dl
                    if step < kh - 1:
                        t_send(slot).start()
                        o_send(slot)[1].start()
                    else:
                        send_or_keep(slot, t_send(slot), sstat, rstat, tr_sem)
                        send_or_keep(slot, o_send(slot)[1], osend, obuf, or_sem)

    with jax.named_scope("twait"):
        for p in range(chips):
            pltpu.make_async_copy(rstat.at[p], rstat.at[p], tr_sem.at[p]).wait()
    peaks = [rstat[p, 0:1, :] for p in range(chips)]
    totals = [rstat[p, 1:2, :] for p in range(chips)]
    peak = functools.reduce(jnp.maximum, peaks)
    shares = [jnp.exp(m - peak) for m in peaks]
    total = sum(s * t for s, t in zip(shares, totals))
    first = (me % g) * nr
    mine = (
        lax.broadcasted_iota(jnp.int32, (nr, HD), 0) + first
        == lax.broadcasted_iota(jnp.int32, (nr, HD), 1)
    )
    shares = [jnp.sum(jnp.where(mine, s / total, 0.0), axis=1, keepdims=True) for s in shares]
    with jax.named_scope("owait"):
        for p in range(chips):
            pltpu.make_async_copy(obuf.at[p], obuf.at[p], or_sem.at[p]).wait()
    with jax.named_scope("wwait"):
        ov_copy.wait()
        for i in range(n):
            w_copy(i).wait()

    with jax.named_scope("project"):
        attended = jnp.zeros((nr, HD), F32)
        for p in range(chips):
            attended = attended + shares[p] * obuf[p].astype(F32)
        a = jnp.concatenate([attended[h * rows:(h + 1) * rows] for h in range(hl)], axis=1).astype(BF16)

        def correct(i, part):
            first_block = dest_of(i) * jb
            return jnp.concatenate(
                [
                    part[:, j * HD:(j + 1) * HD] + cbuf[pl.ds(first_block + j, rows, stride=nblocks), :]
                    for j in range(jb)
                ],
                axis=1,
            )

        def p_send(i):
            return pltpu.make_async_remote_copy(
                src_ref=psend.at[i], dst_ref=precv.at[i], send_sem=ps_sem.at[i], recv_sem=pr_sem.at[i],
                device_id={"tensor": partner}, device_id_type=MESH,
            )

        def s_send(i):
            return pltpu.make_async_remote_copy(
                src_ref=sbuf.at[i], dst_ref=rbuf.at[chip], send_sem=ss_sem.at[i], recv_sem=sr_sem.at[chip],
                device_id={"tensor": 2 * place_of(i) + core}, device_id_type=MESH,
            )

        acc = None
        cross = chips // 2
        groups = [
            [(0, k) for k in range(cross)],
            [(1, 0)] + [(0, k) for k in range(cross, chips)],
            [(1, k) for k in range(1, cross)],
            [(1, k) for k in range(cross, chips - 1)],
            [(1, chips - 1)],
        ]
        for turn, group in enumerate(groups):
            if turn == 0:
                none = jnp.zeros((rows, HD), BF16)
                for h in range(0, hl, 2):
                    pair = jnp.concatenate(
                        [
                            jnp.concatenate([a[:, h * HD:(h + 1) * HD], none], axis=1),
                            jnp.concatenate([none, a[:, (h + 1) * HD:(h + 2) * HD]], axis=1),
                        ],
                        axis=0,
                    )
                    blocks = jnp.concatenate(
                        [jnp.concatenate([ovbuf[h, o], ovbuf[h + 1, o]], axis=0) for o in range(omax)], axis=1
                    )
                    both = jnp.dot(pair, blocks, preferred_element_type=F32)
                    for o in range(omax):
                        for e in range(2):
                            at = ((h + e) * omax + o) * rows
                            tbuf[at:at + rows, :] = both[e * rows:(e + 1) * rows, o * HD:(o + 1) * HD]
                pieces = []
                for r in range(rows):
                    term = tbuf[pl.ds(r, terms, stride=rows), :]
                    high = term.astype(BF16)
                    low = (term - high.astype(F32)).astype(BF16)
                    pieces.append(jnp.concatenate([high, low], axis=0))
                placed = jnp.dot(place[...], jnp.concatenate(pieces, axis=1), preferred_element_type=F32)
                for r in range(rows):
                    cbuf[r * nblocks:(r + 1) * nblocks, :] = placed[:, r * HD:(r + 1) * HD]
            parts = [jnp.dot(a, wbuf[2 * k + keep], preferred_element_type=F32) for keep, k in group]
            parts = [correct(2 * k + keep, part) for (keep, k), part in zip(group, parts)]
            for (keep, k), part in zip(group, parts):
                if not keep:
                    psend[k] = part
            for keep, k in group:
                if not keep:
                    p_send(k).start()
            for (keep, k), part in zip(group, parts):
                if keep:
                    with jax.named_scope("pw%d" % k):
                        p_send(k).wait_recv()
                    part = part + precv[k]
                    if k < chips - 1:
                        sbuf[k] = part.astype(BF16)
                        s_send(k).start()
                    else:
                        acc = part

    with jax.named_scope("gather"):
        for i in range(chips):
            target, copy = q_send(i)
            if i < chips // 2 - window:
                pass
            elif i < chips - 1:
                copy.wait_send()
            else:
                pl.when(target != me)(copy.wait_send)
            target, copy = o_send(i)

            @pl.when(target != me)
            def _():
                copy.wait_send()
                t_send(i).wait_send()

            p_send(i).wait_send()
        for i in range(chips - 1):
            s_send(i).wait_send()
        for mask in range(1, chips):
            p = flip(chip, chip_steps, mask)
            pltpu.make_async_copy(rbuf.at[p], rbuf.at[p], sr_sem.at[p]).wait()
            acc = acc + rbuf[p].astype(F32)
        out_ref[...] = acc.astype(BF16)


def body(n, queries, kv_cache, lengths, out_weight, outlier_values, outlier_columns, outlier_counts):
    rows, width = queries.shape
    hl = width // HD
    nr = hl * rows
    positions = kv_cache.shape[2]
    cols = out_weight.shape[1] // n
    omax = outlier_values.shape[1]
    chips = n // 2
    g = n // KVH
    dma = pltpu.SemaphoreType.DMA
    out = pl.pallas_call(
        functools.partial(kernel, n),
        out_shape=pltpu.VMEM((rows, cols), BF16),
        in_specs=[pl.BlockSpec(memory_space=pl.ANY)] * 7,
        out_specs=pl.BlockSpec(memory_space=pltpu.VMEM),
        scratch_shapes=[
            pltpu.SMEM(lengths.shape, jnp.int32),
            pltpu.SMEM((omax, hl), jnp.int32),
            pltpu.SMEM(outlier_counts.shape, jnp.int32),
            pltpu.VMEM((chips, rows, width), BF16),
            pltpu.VMEM((rows, width), BF16),
            pltpu.VMEM(kv_cache.shape, BF16),
            pltpu.VMEM((2, rows, positions, KVH // 2 * HD), BF16),
            pltpu.VMEM((n, width, cols), BF16),
            pltpu.VMEM(outlier_values.shape, BF16),
            pltpu.VMEM((2, g * nr, rows * positions), F32),
            pltpu.VMEM((2, KVH // 2, HD, rows * positions), BF16),
            pltpu.VMEM((chips, nr, HD), BF16),
            pltpu.VMEM((chips, nr, HD), BF16),
            pltpu.VMEM((chips, 2, HD), F32),
            pltpu.VMEM((chips, 2, HD), F32),
            pltpu.VMEM((hl * omax * rows, HD), F32),
            pltpu.VMEM((n * cols // HD, 2 * hl * omax), BF16),
            pltpu.VMEM((rows * (n * cols // HD), HD), F32),
            pltpu.VMEM((chips, rows, cols), F32),
            pltpu.VMEM((chips, rows, cols), F32),
            pltpu.VMEM((chips, rows, cols), BF16),
            pltpu.VMEM((chips, rows, cols), BF16),
            dma((3,)), dma, dma, dma, dma, dma((chips,)), dma((chips,)), dma((n,)), dma, dma((chips,)), dma((chips,)),
            dma((chips,)), dma((chips,)), dma((chips,)), dma((chips,)), dma((chips,)), dma((chips,)),
        ],
        compiler_params=pltpu.CompilerParams(
            collective_id=0, has_side_effects=True, vmem_limit_bytes=56 * 2**20
        ),
    )(queries, kv_cache, out_weight, outlier_values, lengths, outlier_columns.T, outlier_counts)
    return out


def solution(mesh):
    placed = (
        P("groups", "tensor"),
        P(None, "groups", "tensor", None),
        P("groups"),
        P("tensor", None),
        P("tensor", None, None, None),
        P("tensor", None),
        P("tensor"),
    )
    return jax.shard_map(
        functools.partial(body, mesh.shape["tensor"]),
        mesh=mesh, in_specs=placed, out_specs=P("groups", "tensor"), check_vma=False,
    )
```

```python
import functools
import math

import jax
import jax.numpy as jnp
from jax import lax
from jax.experimental import pallas as pl
from jax.experimental.pallas import tpu as pltpu
from jax.sharding import PartitionSpec as P

KVH = 8
HD = 128
MESH = pl.DeviceIdType.MESH
F32 = jnp.float32
BF16 = jnp.bfloat16


def steps_of(index, n):
    steps, bit = [], 1
    while bit < n:
        steps.append(bit - 2 * bit * ((index // bit) % 2))
        bit *= 2
    return steps


def flip(index, steps, mask):
    for k, step in enumerate(steps):
        if (mask >> k) & 1:
            index = index + step
    return index


def kernel(
    n,
    q_hbm, kv_hbm, w_hbm, ov_hbm, len_hbm, col_hbm, cnt_hbm,
    out_ref,
    len_ref, col_ref, cnt_ref, qbuf, qown, kvown, kvbuf, wbuf, ovbuf, bias, turned, osend, obuf, sstat, rstat, tbuf, place, cbuf,
    psend, precv, sbuf, rbuf,
    small_sem, kv_sem, kvs_sem, kvr_sem, qo_sem, qs_sem, qr_sem, w_sem, ov_sem, os_sem, or_sem, ts_sem, tr_sem,
    ps_sem, pr_sem, ss_sem, sr_sem,
):
    me = lax.axis_index("tensor")
    core = me % 2
    chip = me // 2
    partner = me + 1 - 2 * core
    chips = n // 2
    half = me // chips
    rows, width = q_hbm.shape
    hl = width // HD
    nr = hl * rows
    g = n // KVH
    kh = KVH // 2
    positions = kv_hbm.shape[2]
    cols = w_hbm.shape[1] // n
    omax = ov_hbm.shape[1]
    jb = cols // HD
    hw = kh * HD
    kvcols = rows * positions
    terms = hl * omax
    nblocks = n * jb
    my_slot = me - half * chips
    dev_steps = steps_of(me, n)
    chip_steps = steps_of(chip, chips)

    barrier = pltpu.get_barrier_semaphore()
    slot_steps = steps_of(my_slot, chips)

    def ready(target):
        pl.semaphore_signal(barrier, inc=1, device_id={"tensor": target}, device_id_type=MESH)

    for i in range(chips - 1, 0, -1):
        ready(core * chips + flip(my_slot, slot_steps, i))

    @pl.when(half != core)
    def _():
        ready(core * chips + my_slot)
        ready(partner)

    def far(i):
        return flip(chip, chip_steps, chips - 1 - i)

    other = 1 - (chips - 1 - chip) // (chips - 1)

    def place_of(k):
        if k == chips - 1:
            return chip
        if k == 0:
            return far(0) * (1 - other)
        apart = chips - 1 - chip - k
        return far(k) + other * ((chips * chips - apart * apart) // (chips * chips)) * (far(0) - far(k))

    def dest_of(i):
        return 2 * place_of(i // 2) + (core + 1 + i % 2) % 2

    q_stage = pltpu.make_async_copy(q_hbm, qown, qo_sem)
    q_stage.start()
    kv_own = pltpu.make_async_copy(kv_hbm, kvown, kv_sem)
    kv_own.start()
    small = [
        pltpu.make_async_copy(src, dst, small_sem.at[i])
        for i, (src, dst) in enumerate(((len_hbm, len_ref), (col_hbm, col_ref), (cnt_hbm, cnt_ref)))
    ]
    for copy in small:
        copy.start()

    swap = pltpu.make_async_remote_copy(
        src_ref=kvown.at[:, :, :, pl.ds(pl.multiple_of((1 - core) * hw, hw), hw)], dst_ref=kvbuf, send_sem=kvs_sem, recv_sem=kvr_sem,
        device_id={"tensor": partner}, device_id_type=MESH,
    )

    def q_send(i):
        target = 2 * far(i) + half
        return target, pltpu.make_async_remote_copy(
            src_ref=qown, dst_ref=qbuf.at[my_slot], send_sem=qs_sem.at[i], recv_sem=qr_sem.at[my_slot],
            device_id={"tensor": target}, device_id_type=MESH,
        )

    def w_copy(i):
        return pltpu.make_async_copy(
            w_hbm.at[:, pl.ds(pl.multiple_of(dest_of(i) * cols, cols), cols)], wbuf.at[i], w_sem.at[i]
        )

    ov_copy = pltpu.make_async_copy(ov_hbm, ovbuf, ov_sem)

    @pl.when(me < n)
    def _():
        ov_copy.start()
        for i in range(n):
            w_copy(i).start()

    with jax.named_scope("barrier"):
        q_stage.wait()
        pl.semaphore_wait(barrier, chips)

    apart = chips // 2
    window = 3

    def q_start(i):
        target, copy = q_send(i)
        if i < chips - 1:
            copy.start()
        else:
            pl.when(target != me)(copy.start)

    for i in range(window):
        q_start(i)
    kv_own.wait()
    swap.start()

    @pl.when(half == core)
    def _():
        pltpu.make_async_copy(qown, qbuf.at[my_slot], qr_sem.at[my_slot]).start()

    with jax.named_scope("pace"):
        for i in range(window, apart):
            q_send(i - window)[1].wait_send()
            q_start(i)
        for i in range(apart, chips):
            q_start(i)

    with jax.named_scope("masks"):
        for copy in small:
            copy.wait()
        rowreq = lax.broadcasted_iota(jnp.int32, (g * nr, kvcols), 0) % rows
        colidx = lax.broadcasted_iota(jnp.int32, (1, kvcols), 1)
        colreq = colidx // positions
        limit = jnp.zeros((1, kvcols), jnp.int32)
        for r in range(rows):
            limit = jnp.where(colreq == r, len_ref[r], limit)
        for part in range(2):
            dev = me if part == 0 else partner
            live = (colidx % positions + dev * positions) < limit
            tag = jnp.where(live, colreq, -1)
            bias[part] = jnp.where(rowreq == tag, 0.0, -1e30).astype(F32)
        lane = lax.broadcasted_iota(jnp.int32, (nblocks, 2 * terms), 1) % terms
        row = lax.broadcasted_iota(jnp.int32, (nblocks, 2 * terms), 0)
        wanted = jnp.full((nblocks, 2 * terms), -1, jnp.int32)
        for h in range(hl):
            for o in range(omax):
                wanted = jnp.where(lane == h * omax + o, jnp.where(o < cnt_ref[h], col_ref[o, h], -1), wanted)
        place[...] = jnp.where(wanted == row, 1.0, 0.0).astype(BF16)

    with jax.named_scope("turn"):
        for kl in range(kh):
            own_lanes = pl.ds(pl.multiple_of(core * hw + kl * HD, HD), HD)
            turned[0, kl] = kvown[0, :, :, own_lanes].reshape(kvcols, HD).T
    with jax.named_scope("kvwait"):
        swap.wait()
    with jax.named_scope("turn2"):
        for kl in range(kh):
            turned[1, kl] = kvbuf[0, :, :, pl.ds(kl * HD, HD)].reshape(kvcols, HD).T

    eye = lax.broadcasted_iota(jnp.int32, (g * nr, HD), 0) == lax.broadcasted_iota(jnp.int32, (g * nr, HD), 1)

    def to_row(column):
        return jnp.sum(jnp.where(eye, column, 0.0), axis=0, keepdims=True)

    def o_send(j):
        target = core * chips + j
        return target, pltpu.make_async_remote_copy(
            src_ref=osend.at[j], dst_ref=obuf.at[chip], send_sem=os_sem.at[j], recv_sem=or_sem.at[chip],
            device_id={"tensor": target}, device_id_type=MESH,
        )

    def t_send(j):
        return pltpu.make_async_remote_copy(
            src_ref=sstat.at[j], dst_ref=rstat.at[chip], send_sem=ts_sem.at[j], recv_sem=tr_sem.at[chip],
            device_id={"tensor": core * chips + j}, device_id_type=MESH,
        )

    def send_or_keep(j, remote, src, dst, sem):
        target = core * chips + j

        @pl.when(target != me)
        def _():
            remote.start()

        @pl.when(target == me)
        def _():
            pltpu.make_async_copy(src.at[j], dst.at[chip], sem.at[chip]).start()

    kl_here = (chip * 2 // g) % kh
    kl_steps = steps_of(kl_here, kh)
    def attend(kl):
        own_lanes = pl.ds(pl.multiple_of(core * hw + kl * HD, HD), HD)
        lanes = pl.ds(pl.multiple_of(kl * HD, HD), HD)
        pieces = []
        for dl in range(g):
            got = qbuf[kl * g + dl].astype(F32)
            pieces += [got[:, h * HD:(h + 1) * HD] for h in range(hl)]
        q = jnp.concatenate(pieces, axis=0).astype(BF16)
        scores, values = [], []
        for part in range(2):
            held, at = (kvown, own_lanes) if part == 0 else (kvbuf, lanes)
            values.append(held[1, :, :, at].reshape(kvcols, HD))
            s = jnp.dot(q, turned[part, kl], preferred_element_type=F32)
            scores.append(s * (1.0 / math.sqrt(HD)) + bias[part])
        peak = jnp.max(jnp.maximum(scores[0], scores[1]), axis=-1, keepdims=True)
        peak = jnp.maximum(peak, -(2.0**66))
        raised = [jnp.exp(s - peak) for s in scores]
        total = jnp.sum(raised[0] + raised[1], axis=-1, keepdims=True)
        o = jnp.dot(raised[0].astype(BF16), values[0], preferred_element_type=F32)
        o = o + jnp.dot(raised[1].astype(BF16), values[1], preferred_element_type=F32)
        stats = jnp.concatenate([to_row(peak), to_row(total)], axis=0)
        return stats, o.astype(BF16)

    per = 1
    with jax.named_scope("attention"):
        for group in range(0, kh, per):
            kls = [flip(kl_here, kl_steps, kh - 1 - step) for step in range(group, group + per)]
            with jax.named_scope("qw%d" % group):
                for kl in kls:
                    for dl in range(g):
                        slot = kl * g + dl
                        pltpu.make_async_copy(qbuf.at[slot], qbuf.at[slot], qr_sem.at[slot]).wait()
            found = [attend(kl) for kl in kls]
            for kl, (stats, o) in zip(kls, found):
                for dl in range(g):
                    sstat[kl * g + dl] = stats
                    osend[kl * g + dl] = o[dl * nr:(dl + 1) * nr]
            for step, kl in zip(range(group, group + per), kls):
                for dl in range(g):
                    slot = kl * g + dl
                    if step < kh - 1:
                        t_send(slot).start()
                        o_send(slot)[1].start()
                    else:
                        send_or_keep(slot, t_send(slot), sstat, rstat, tr_sem)
                        send_or_keep(slot, o_send(slot)[1], osend, obuf, or_sem)

    with jax.named_scope("twait"):
        for p in range(chips):
            pltpu.make_async_copy(rstat.at[p], rstat.at[p], tr_sem.at[p]).wait()
    peaks = [rstat[p, 0:1, :] for p in range(chips)]
    totals = [rstat[p, 1:2, :] for p in range(chips)]
    peak = functools.reduce(jnp.maximum, peaks)
    shares = [jnp.exp(m - peak) for m in peaks]
    total = sum(s * t for s, t in zip(shares, totals))
    first = (me % g) * nr
    mine = (
        lax.broadcasted_iota(jnp.int32, (nr, HD), 0) + first
        == lax.broadcasted_iota(jnp.int32, (nr, HD), 1)
    )
    shares = [jnp.sum(jnp.where(mine, s / total, 0.0), axis=1, keepdims=True) for s in shares]
    with jax.named_scope("owait"):
        for p in range(chips):
            pltpu.make_async_copy(obuf.at[p], obuf.at[p], or_sem.at[p]).wait()
    with jax.named_scope("wwait"):
        ov_copy.wait()
        for i in range(n):
            w_copy(i).wait()

    with jax.named_scope("project"):
        attended = jnp.zeros((nr, HD), F32)
        for p in range(chips):
            attended = attended + shares[p] * obuf[p].astype(F32)
        a = jnp.concatenate([attended[h * rows:(h + 1) * rows] for h in range(hl)], axis=1).astype(BF16)

        def correct(i, part):
            first_block = dest_of(i) * jb
            return jnp.concatenate(
                [
                    part[:, j * HD:(j + 1) * HD] + cbuf[pl.ds(first_block + j, rows, stride=nblocks), :]
                    for j in range(jb)
                ],
                axis=1,
            )

        def p_send(i):
            return pltpu.make_async_remote_copy(
                src_ref=psend.at[i], dst_ref=precv.at[i], send_sem=ps_sem.at[i], recv_sem=pr_sem.at[i],
                device_id={"tensor": partner}, device_id_type=MESH,
            )

        def s_send(i):
            return pltpu.make_async_remote_copy(
                src_ref=sbuf.at[i], dst_ref=rbuf.at[chip], send_sem=ss_sem.at[i], recv_sem=sr_sem.at[chip],
                device_id={"tensor": 2 * place_of(i) + core}, device_id_type=MESH,
            )

        acc = None
        cross = chips // 2
        groups = [
            [(0, k) for k in range(cross)],
            [(1, 0)] + [(0, k) for k in range(cross, chips - 1)],
            [(1, k) for k in range(1, cross)] + [(0, chips - 1)],
            [(1, k) for k in range(cross, chips - 1)],
            [(1, chips - 1)],
        ]
        for turn, group in enumerate(groups):
            if turn == 0:
                none = jnp.zeros((rows, HD), BF16)
                for h in range(0, hl, 2):
                    pair = jnp.concatenate(
                        [
                            jnp.concatenate([a[:, h * HD:(h + 1) * HD], none], axis=1),
                            jnp.concatenate([none, a[:, (h + 1) * HD:(h + 2) * HD]], axis=1),
                        ],
                        axis=0,
                    )
                    blocks = jnp.concatenate(
                        [jnp.concatenate([ovbuf[h, o], ovbuf[h + 1, o]], axis=0) for o in range(omax)], axis=1
                    )
                    both = jnp.dot(pair, blocks, preferred_element_type=F32)
                    for o in range(omax):
                        for e in range(2):
                            at = ((h + e) * omax + o) * rows
                            tbuf[at:at + rows, :] = both[e * rows:(e + 1) * rows, o * HD:(o + 1) * HD]
                pieces = []
                for r in range(rows):
                    term = tbuf[pl.ds(r, terms, stride=rows), :]
                    high = term.astype(BF16)
                    low = (term - high.astype(F32)).astype(BF16)
                    pieces.append(jnp.concatenate([high, low], axis=0))
                placed = jnp.dot(place[...], jnp.concatenate(pieces, axis=1), preferred_element_type=F32)
                for r in range(rows):
                    cbuf[r * nblocks:(r + 1) * nblocks, :] = placed[:, r * HD:(r + 1) * HD]
            parts = [jnp.dot(a, wbuf[2 * k + keep], preferred_element_type=F32) for keep, k in group]
            parts = [correct(2 * k + keep, part) for (keep, k), part in zip(group, parts)]
            for (keep, k), part in zip(group, parts):
                if not keep:
                    psend[k] = part
            for keep, k in group:
                if not keep:
                    p_send(k).start()
            for (keep, k), part in zip(group, parts):
                if keep:
                    with jax.named_scope("pw%d" % k):
                        p_send(k).wait_recv()
                    part = part + precv[k]
                    if k < chips - 1:
                        sbuf[k] = part.astype(BF16)
                        s_send(k).start()
                    else:
                        acc = part

    with jax.named_scope("gather"):
        for i in range(chips):
            target, copy = q_send(i)
            if i < chips // 2 - window:
                pass
            elif i < chips - 1:
                copy.wait_send()
            else:
                pl.when(target != me)(copy.wait_send)
            target, copy = o_send(i)

            @pl.when(target != me)
            def _():
                copy.wait_send()
                t_send(i).wait_send()

            p_send(i).wait_send()
        for i in range(chips - 1):
            s_send(i).wait_send()
        for mask in range(1, chips):
            p = flip(chip, chip_steps, mask)
            pltpu.make_async_copy(rbuf.at[p], rbuf.at[p], sr_sem.at[p]).wait()
            acc = acc + rbuf[p].astype(F32)
        out_ref[...] = acc.astype(BF16)


def body(n, queries, kv_cache, lengths, out_weight, outlier_values, outlier_columns, outlier_counts):
    rows, width = queries.shape
    hl = width // HD
    nr = hl * rows
    positions = kv_cache.shape[2]
    cols = out_weight.shape[1] // n
    omax = outlier_values.shape[1]
    chips = n // 2
    g = n // KVH
    dma = pltpu.SemaphoreType.DMA
    out = pl.pallas_call(
        functools.partial(kernel, n),
        out_shape=pltpu.VMEM((rows, cols), BF16),
        in_specs=[pl.BlockSpec(memory_space=pl.ANY)] * 7,
        out_specs=pl.BlockSpec(memory_space=pltpu.VMEM),
        scratch_shapes=[
            pltpu.SMEM(lengths.shape, jnp.int32),
            pltpu.SMEM((omax, hl), jnp.int32),
            pltpu.SMEM(outlier_counts.shape, jnp.int32),
            pltpu.VMEM((chips, rows, width), BF16),
            pltpu.VMEM((rows, width), BF16),
            pltpu.VMEM(kv_cache.shape, BF16),
            pltpu.VMEM((2, rows, positions, KVH // 2 * HD), BF16),
            pltpu.VMEM((n, width, cols), BF16),
            pltpu.VMEM(outlier_values.shape, BF16),
            pltpu.VMEM((2, g * nr, rows * positions), F32),
            pltpu.VMEM((2, KVH // 2, HD, rows * positions), BF16),
            pltpu.VMEM((chips, nr, HD), BF16),
            pltpu.VMEM((chips, nr, HD), BF16),
            pltpu.VMEM((chips, 2, HD), F32),
            pltpu.VMEM((chips, 2, HD), F32),
            pltpu.VMEM((hl * omax * rows, HD), F32),
            pltpu.VMEM((n * cols // HD, 2 * hl * omax), BF16),
            pltpu.VMEM((rows * (n * cols // HD), HD), F32),
            pltpu.VMEM((chips, rows, cols), F32),
            pltpu.VMEM((chips, rows, cols), F32),
            pltpu.VMEM((chips, rows, cols), BF16),
            pltpu.VMEM((chips, rows, cols), BF16),
            dma((3,)), dma, dma, dma, dma, dma((chips,)), dma((chips,)), dma((n,)), dma, dma((chips,)), dma((chips,)),
            dma((chips,)), dma((chips,)), dma((chips,)), dma((chips,)), dma((chips,)), dma((chips,)),
        ],
        compiler_params=pltpu.CompilerParams(
            collective_id=0, has_side_effects=True, vmem_limit_bytes=56 * 2**20
        ),
    )(queries, kv_cache, out_weight, outlier_values, lengths, outlier_columns.T, outlier_counts)
    return out


def solution(mesh):
    placed = (
        P("groups", "tensor"),
        P(None, "groups", "tensor", None),
        P("groups"),
        P("tensor", None),
        P("tensor", None, None, None),
        P("tensor", None),
        P("tensor"),
    )
    return jax.shard_map(
        functools.partial(body, mesh.shape["tensor"]),
        mesh=mesh, in_specs=placed, out_specs=P("groups", "tensor"), check_vma=False,
    )
```
